256 devices in a mesh: node: 64 (over z, y, core), feat: 4 (over x).
Axes of the slice: x: 4, y: 4, z: 8, core: 2. Of those that a mesh axis runs over, the one named last changes fastest.
Arguments:
- features: bfloat16 [262144, 256], P(('node', 'feat')), may hold values from -6 to 6
- weight: bfloat16 [256, 256], replicated, may hold values from -1.5 to 1.5
- grad_out: bfloat16 [262144, 256], P(('node', 'feat')), may hold values from -6 to 6
- local_rows: int32 [64, 4, 32], P('node', 'feat'), may hold values from 0 to 7
- local_cols: int32 [64, 4, 32], P('node', 'feat'), may hold values from 0 to 31
- local_values: bfloat16 [64, 4, 32, 128, 128], P('node', 'feat'), may hold values from 0 to 3, as said below
- remote_rows: int32 [64, 4, 3, 16], P('node', 'feat'), may hold values from 0 to 7
- remote_slots: int32 [64, 4, 3, 16], P('node', 'feat'), may hold values from 0 to 15
- remote_values: bfloat16 [64, 4, 3, 16, 128, 128], P('node', 'feat'), may hold values from 0 to 3, as said below
- send_blocks: int32 [64, 3, 16], P('node'), may hold values from 0 to 31, as said below
- tile_counts: int32 [64, 4, 4], P('node', 'feat'), may hold values from 1 to 32, as said below
Outputs:
- output: bfloat16 [262144, 256], P(('node', 'feat'))
- grad_features: bfloat16 [262144, 256], P(('node', 'feat'))
The draws below stay inside these ranges and needn't reach their ends.
Inputs may be any that keep to these rules, and one draw needn't show every extreme that they name: `tile_counts`: column 0 is at most 32 and every other column at most 16; each column reaches its bound on some device, and other devices hold all, a half or a quarter of it, at least 1. `send_blocks`: the 16 blocks of one part and round are distinct. `local_values`: each entry is zero or a positive edge weight. `remote_values`: each entry is zero or a positive edge weight.
All inputs are finite; a program needn't handle non-finite values.
Results may differ from the reference program's by a relative error of at most 0.0049.
Values may be sent and summed in bfloat16 or wider, within the bound.
No kernel may reach another device: no remote copies, remote signals or barrier semaphores. Data moves between devices by JAX's collectives and lax.ppermute only.
A program may use at most 128 MiB of HBM per device.

```python
import jax
import jax.numpy as jnp
from jax import lax

F = 256
BLOCK = 128
BLOCKS_DEV = 8
ROUNDS = 3
BLOCKS_PART = 32
NEED = 16
LOCAL_CAP = 32
REMOTE_CAP = 16
PARTS_SIZE = 64
NODES = 262144
N_NODE = 64
N_FEAT = 4


def tile_draw(key, shape):
    key_mask, key_value = jax.random.split(key)
    kept_mask = jax.random.randint(key_mask, shape, 0, BLOCK) < 4
    weights = jnp.exp(jax.random.uniform(key_value, shape, jnp.float32, -0.7, 0.7))
    return jnp.where(kept_mask, weights, jnp.float32(0.0)).astype(jnp.bfloat16)


def draw_local_values(key, part):
    return tile_draw(key, (PARTS_SIZE, N_FEAT, LOCAL_CAP, BLOCK, BLOCK))


def draw_remote_values(key, part):
    return tile_draw(key, (PARTS_SIZE, N_FEAT, ROUNDS, REMOTE_CAP, BLOCK, BLOCK))


def pick_blocks(single_key):
    return jax.random.permutation(single_key, BLOCKS_PART)[:NEED]


def draw_send_blocks(key, part):
    all_keys = jax.random.split(key, PARTS_SIZE * ROUNDS)
    picked = jax.vmap(pick_blocks)(all_keys)
    return picked.reshape(PARTS_SIZE, ROUNDS, NEED).astype(jnp.int32)


def draw_tile_counts(key, part):
    key_shift, key_top = jax.random.split(key)
    device_count = PARTS_SIZE * N_FEAT
    shifts = jax.random.randint(key_shift, (device_count, ROUNDS + 1), 0, 3)
    limits = jnp.concatenate([jnp.full((1,), LOCAL_CAP, jnp.int32), jnp.full((ROUNDS,), REMOTE_CAP, jnp.int32)])
    divisor = jnp.left_shift(jnp.ones((device_count, ROUNDS + 1), jnp.int32), shifts)
    counts = jnp.maximum(limits[None, :] // divisor, 1)
    topmost = jax.random.randint(key_top, (ROUNDS + 1,), 0, device_count)
    device_ids = jnp.arange(device_count, dtype=jnp.int32)
    counts = jnp.where(device_ids[:, None] == topmost[None, :], limits[None, :], counts)
    return counts.reshape(PARTS_SIZE, N_FEAT, ROUNDS + 1).astype(jnp.int32)


def with_ends(values, rng, least, high):
    longest = values.shape.index(max(values.shape))
    spots = []
    for shift in (0, 1):
        where = [jax.random.randint(jax.random.fold_in(rng, axis), (), 0, length) for axis, length in enumerate(values.shape)]
        where[longest] = (where[longest] + shift) % values.shape[longest]
        spots.append(tuple(where))
    return values.at[spots[0]].set(least).at[spots[1]].set(high)


def level_of(stream_key, extent, pieces, smallest, top_value):
    def one(position, shards_of):
        steps = jax.random.uniform(jax.random.fold_in(jax.random.fold_in(stream_key, 6), position), (shards_of,), jnp.float32, smallest / len(pieces), top_value / len(pieces))
        return jnp.repeat(jnp.exp(steps), extent[position] // shards_of).reshape((-1,) + (1,) * (len(extent) - position - 1))

    gain = one(*pieces[0])
    for cut in pieces[1:]:
        gain = gain * one(*cut)
    return gain


def normal_values(own_key, shape, scale, limit, shards=(), kind=jnp.bfloat16):
    result = scale * jax.random.normal(own_key, shape, jnp.float32)
    if shards:
        result = result * level_of(own_key, shape, shards, -0.22, 0.18)
    return jnp.clip(result, -limit, limit).astype(kind)


def setup_inputs(seed: int = 0) -> dict:
    arg_keys = jax.random.split(jax.random.key(seed), 12)
    features = normal_values(arg_keys[0], (NODES, F), 1.0, 6.0, ((0, 256),))
    weight = normal_values(arg_keys[1], (F, F), (F // 16) ** -0.5, 1.5)
    grad_out = normal_values(arg_keys[2], (NODES, F), 1.0, 6.0, ((0, 256),))
    local_rows = with_ends(jax.random.randint(arg_keys[3], (PARTS_SIZE, N_FEAT, LOCAL_CAP), 0, BLOCKS_DEV), jax.random.fold_in(arg_keys[3], 1), 0, BLOCKS_DEV - 1).astype(jnp.int32)
    local_cols = with_ends(jax.random.randint(arg_keys[4], (PARTS_SIZE, N_FEAT, LOCAL_CAP), 0, BLOCKS_PART), jax.random.fold_in(arg_keys[4], 1), 0, BLOCKS_PART - 1).astype(jnp.int32)
    local_values = draw_local_values(jax.random.fold_in(arg_keys[11], 71), 0)
    remote_rows = with_ends(jax.random.randint(arg_keys[6], (PARTS_SIZE, N_FEAT, ROUNDS, REMOTE_CAP), 0, BLOCKS_DEV), jax.random.fold_in(arg_keys[6], 1), 0, BLOCKS_DEV - 1).astype(jnp.int32)
    remote_slots = with_ends(jax.random.randint(arg_keys[7], (PARTS_SIZE, N_FEAT, ROUNDS, REMOTE_CAP), 0, NEED), jax.random.fold_in(arg_keys[7], 1), 0, NEED - 1).astype(jnp.int32)
    remote_values = draw_remote_values(jax.random.fold_in(arg_keys[11], 71), 0)
    send_blocks = draw_send_blocks(jax.random.fold_in(arg_keys[11], 71), 0)
    tile_counts = draw_tile_counts(jax.random.fold_in(arg_keys[11], 71), 0)
    return dict(features=features, weight=weight, grad_out=grad_out, local_rows=local_rows, local_cols=local_cols, local_values=local_values, remote_rows=remote_rows, remote_slots=remote_slots, remote_values=remote_values, send_blocks=send_blocks, tile_counts=tile_counts)


def part_blocks(table, part_id):
    rows = BLOCKS_PART * BLOCK
    piece = lax.dynamic_slice_in_dim(table, (part_id * rows).astype(jnp.int32), rows, 0)
    return piece.reshape(BLOCKS_PART, BLOCK, F)


def spread(one_hot, values):
    return jnp.einsum('tb,tif->bif', one_hot, values, precision=lax.Precision.HIGHEST)


def block_hot(targets, live):
    block_ids = jnp.arange(BLOCKS_PART, dtype=jnp.int32)
    return ((targets[:, None] == block_ids[None, :]) & live[:, None]).astype(jnp.float32)


def round_bits():
    log_nodes = int(N_NODE).bit_length() - 1
    return [(round_no * log_nodes) // ROUNDS for round_no in range(ROUNDS)]


def reference(features, weight, grad_out, local_rows, local_cols, local_values, remote_rows, remote_slots, remote_values, send_blocks, tile_counts):
    bits = round_bits()
    part_ids = jnp.arange(PARTS_SIZE, dtype=jnp.int32)
    offsets = (jnp.arange(N_FEAT, dtype=jnp.int32) * BLOCKS_DEV)[:, None]
    local_slot = jnp.arange(LOCAL_CAP, dtype=jnp.int32)[None, :]
    remote_slot = jnp.arange(REMOTE_CAP, dtype=jnp.int32)[None, :]

    def forward(part_id):
        own = part_blocks(features, part_id).astype(jnp.float32)
        counts = tile_counts[part_id]
        dests = (local_rows[part_id] + offsets).reshape(-1)
        sources_ids = local_cols[part_id].reshape(-1)
        tile_vals = local_values[part_id].astype(jnp.float32).reshape(-1, BLOCK, BLOCK)
        live = (local_slot < counts[:, 0:1]).reshape(-1)
        one_hot = block_hot(dests, live)
        product = jnp.einsum('tij,tjf->tif', tile_vals, own[sources_ids], precision=lax.Precision.HIGHEST)
        totals = own + spread(one_hot, product)
        rowsum = jnp.einsum('tb,ti->bi', one_hot, jnp.sum(tile_vals, axis=-1), precision=lax.Precision.HIGHEST)
        for round_no, bit_no in enumerate(bits):
            partner = jnp.bitwise_xor(part_id, jnp.int32(1 << bit_no))
            source_ids = send_blocks[partner, round_no][remote_slots[part_id, :, round_no]].reshape(-1)
            sources = part_blocks(features, partner).astype(jnp.float32)[source_ids]
            rvals = remote_values[part_id, :, round_no].astype(jnp.float32).reshape(-1, BLOCK, BLOCK)
            rlive = (remote_slot < counts[:, round_no + 1:round_no + 2]).reshape(-1)
            rdests = (remote_rows[part_id, :, round_no] + offsets).reshape(-1)
            rhot = block_hot(rdests, rlive)
            rprod = jnp.einsum('tij,tjf->tif', rvals, sources, precision=lax.Precision.HIGHEST)
            totals = totals + spread(rhot, rprod)
            rowsum = rowsum + jnp.einsum('tb,ti->bi', rhot, jnp.sum(rvals, axis=-1), precision=lax.Precision.HIGHEST)
        degree = 1.0 + rowsum
        hidden = (totals / degree[:, :, None]).astype(jnp.bfloat16)
        return hidden, degree

    hidden, degree = lax.map(forward, part_ids)
    hidden = hidden.reshape(NODES, F)
    degree = degree.reshape(NODES)
    output = jnp.dot(hidden, weight, preferred_element_type=jnp.float32).astype(jnp.bfloat16)
    grad_dense = jnp.dot(grad_out, weight.T, preferred_element_type=jnp.float32)
    grad_hidden = (grad_dense / degree[:, None]).astype(jnp.bfloat16)

    def backward(part_id):
        own = part_blocks(grad_hidden, part_id).astype(jnp.float32)
        counts = tile_counts[part_id]
        dests = (local_rows[part_id] + offsets).reshape(-1)
        sources_ids = local_cols[part_id].reshape(-1)
        tile_vals = local_values[part_id].astype(jnp.float32).reshape(-1, BLOCK, BLOCK)
        live = (local_slot < counts[:, 0:1]).reshape(-1)
        back = jnp.einsum('tij,tif->tjf', tile_vals, own[dests], precision=lax.Precision.HIGHEST)
        grad_sum = own + spread(block_hot(sources_ids, live), back)
        for round_no, bit_no in enumerate(bits):
            partner = jnp.bitwise_xor(part_id, jnp.int32(1 << bit_no))
            peer_grad = part_blocks(grad_hidden, partner).astype(jnp.float32)
            pvals = remote_values[partner, :, round_no].astype(jnp.float32).reshape(-1, BLOCK, BLOCK)
            plive = (remote_slot < tile_counts[partner, :, round_no + 1:round_no + 2]).reshape(-1)
            pdests = (remote_rows[partner, :, round_no] + offsets).reshape(-1)
            pback = jnp.einsum('tij,tif->tjf', pvals, peer_grad[pdests], precision=lax.Precision.HIGHEST)
            targets = send_blocks[part_id, round_no][remote_slots[partner, :, round_no].reshape(-1)]
            grad_sum = grad_sum + spread(block_hot(targets, plive), pback)
        return grad_sum.astype(jnp.bfloat16)

    grad_features = lax.map(backward, part_ids).reshape(NODES, F)
    return output, grad_features
```

```python
import jax
import jax.numpy as jnp
from jax import lax
from jax.experimental import pallas as pl
from jax.experimental.pallas import tpu as pltpu
from jax.sharding import PartitionSpec as P

UNROLL = 4
F32 = jnp.float32
BF16 = jnp.bfloat16
SMEM = pl.BlockSpec(memory_space=pltpu.SMEM)
VMEM = pl.BlockSpec(memory_space=pltpu.VMEM)
ANY = pl.BlockSpec(memory_space=pl.ANY)


def swapped(array, bit):
    return lax.ppermute(array, "node", [(i, i ^ 1 << bit) for i in range(lax.axis_size("node"))])


def shifted(array, step):
    size = lax.axis_size("feat")
    return lax.ppermute(array, "feat", [(i, (i + step) % size) for i in range(size)])


def spread_out(mine):
    half = mine.shape[0] // 2
    before = shifted(mine, 1)
    after = shifted(mine, -1)
    far_low = shifted(before[:half], 1)
    far_high = shifted(after[half:], -1)
    return (mine, after, far_low, far_high, before)


def start_all(pairs, sems):
    copies = [pltpu.make_async_copy(a, b, sems.at[i]) for i, (a, b) in enumerate(pairs)]
    for copy in copies:
        copy.start()
    return copies


def wait_all(copies):
    for copy in copies:
        copy.wait()


def pieces_into(pieces, dst, base):
    pairs = []
    for piece in pieces:
        pairs.append((piece, dst.at[pl.ds(base, piece.shape[0])]))
        base += piece.shape[0]
    return pairs


def for_live(count, step):
    def group(k, carry):
        for u in range(UNROLL):
            t = k * UNROLL + u
            step(t, t < count)
        return carry

    lax.fori_loop(0, pl.cdiv(count, UNROLL), group, 0)


def forward_tiles(count, base, vals, row_of, source_of, acc):
    trash = acc.shape[0] - 1

    def step(t, live):
        row = jnp.where(live, row_of(t), trash)
        acc[row] += jnp.dot(vals[base + t], source_of(t), preferred_element_type=F32)

    for_live(count, step)


def backward_tiles(count, base, vals, row_of, target_of, grads, acc):
    trash = acc.shape[0] - 1

    def step(t, live):
        target = jnp.where(live, target_of(t), trash)
        acc[target] += lax.dot_general(
            vals[base + t], grads[row_of(t)], (((0,), (0,)), ((), ())), preferred_element_type=F32
        )

    for_live(count, step)


def degree_kernel(counts, lrows, rrows, rslots, me, lv_hbm, rv_hbm, go_hbm, w_ref,
                  deg_ref, gh_ref, right_ref, left_ref, keep_r_ref, keep_l_ref, own_ref,
                  lv, rv, go, dacc, acc, sems):
    copies = start_all([(lv_hbm, lv), (rv_hbm, rv), (go_hbm, go)], sems)
    own = deg_ref.shape[0]
    cap = rrows.shape[1]
    dacc[...] = jnp.zeros_like(dacc)
    acc[...] = jnp.zeros_like(acc)
    copies[0].wait()

    def add_rows(vals, base, row_of):
        def step(t, live):
            row = jnp.where(live, row_of(t), own)
            dacc[row] += vals[base + t].astype(F32)
        return step

    for_live(counts[0], add_rows(lv, 0, lambda t: lrows[t]))
    copies[1].wait()
    for r in range(rrows.shape[0]):
        for_live(counts[r + 1], add_rows(rv, r * cap, lambda t: rrows[r, t]))
    copies[2].wait()
    for b in range(own):
        degree = 1.0 + jnp.broadcast_to(jnp.sum(dacc[b], axis=1, keepdims=True), dacc.shape[1:])
        deg_ref[b] = degree
        dense = lax.dot_general(go[b], w_ref[...], (((1,), (1,)), ((), ())), preferred_element_type=F32)
        width = degree.shape[1]
        for k in range(dense.shape[1] // width):
            gh_ref[b, :, k * width:(k + 1) * width] = (
                dense[:, k * width:(k + 1) * width] / degree
            ).astype(BF16)
    last = rrows.shape[0] - 1
    share = own_ref.shape[0]
    shift = me[0] * share
    backward_tiles(
        counts[last + 1], last * cap, rv, lambda t: rrows[last, t],
        lambda t: lax.rem(rslots[last, t] - shift + cap, cap), gh_ref, acc,
    )
    split_out(acc, share, right_ref, left_ref, keep_r_ref, keep_l_ref, own_ref)


def split_out(acc, n, right_ref, left_ref, keep_r_ref, keep_l_ref, own_ref):
    h = n // 2
    right_ref[:h] = acc[2 * n:2 * n + h].astype(BF16)
    right_ref[h:] = acc[n + h:2 * n].astype(BF16)
    left_ref[:h] = acc[2 * n + h:3 * n].astype(BF16)
    left_ref[h:] = acc[3 * n:3 * n + h].astype(BF16)
    keep_r_ref[...] = acc[n:n + h]
    keep_l_ref[...] = acc[3 * n + h:4 * n]
    own_ref[...] = acc[:n]


def parcels_kernel(counts, rrows, rslots, rv_ref, gh_ref, out_a, out_b, acc):
    cap = rrows.shape[1]
    for r, out in ((1, out_b), (0, out_a)):
        acc[...] = jnp.zeros_like(acc)
        backward_tiles(
            counts[r + 1], r * cap, rv_ref, lambda t: rrows[r, t], lambda t: rslots[r, t], gh_ref, acc
        )
        out[...] = acc[:out.shape[0]].astype(BF16)


def local_back_kernel(counts, lrows, lcols, me, lv_ref, gh_ref, out_ref, acc):
    total = out_ref.shape[0]
    own = gh_ref.shape[0]
    acc[...] = jnp.zeros_like(acc)
    shift = me[0] * own
    backward_tiles(
        counts[0], 0, lv_ref, lambda t: lrows[t],
        lambda t: lax.rem(lcols[t] - shift + total, total), gh_ref, acc,
    )
    acc[:own] += gh_ref[...].astype(F32)
    out_ref[...] = acc[:total]


def combine_kernel(keep_r, keep_l, from_left, from_right, out_r, out_l):
    h = keep_r.shape[0]
    out_r[...] = (keep_r[...] + from_left[:h].astype(F32)).astype(BF16)
    out_l[...] = (keep_l[...] + from_right[:h].astype(F32)).astype(BF16)


def finish_kernel(own, a_left, a_right, b_left, b_right, out):
    h = own.shape[0] // 2
    out[:h] = (own[:h] + a_right[h:].astype(F32) + b_left[...].astype(F32)).astype(BF16)
    out[h:] = (own[h:] + a_left[h:].astype(F32) + b_right[...].astype(F32)).astype(BF16)


def merge_kernel(sends, me, part_hbm, got_a, got_b, got_c,
                 right_ref, left_ref, keep_r_ref, keep_l_ref, own_ref, acc, sems):
    copies = start_all([(part_hbm, acc)], sems)
    total = acc.shape[0]
    own = own_ref.shape[0]
    shift = me[0] * own
    wait_all(copies)

    def add(got, r, base):
        for s in range(got.shape[0]):
            block = lax.rem(sends[r, base + s] - shift + total, total)
            acc[block] += got[s].astype(F32)

    add(got_a, 0, 0)
    add(got_b, 1, 0)
    add(got_c, 2, me[0] * got_c.shape[0])
    split_out(acc, own, right_ref, left_ref, keep_r_ref, keep_l_ref, own_ref)


def pick_kernel(sends, me, p0, p1, p2, p3, p4, out_a, out_b, out_c, src, sems):
    pieces = (p0, p1, p2, p3, p4)
    wait_all(start_all(pieces_into(pieces, src, 0), sems))
    total = src.shape[0]
    shift = me[0] * p0.shape[0]

    def put(out, r, base):
        for s in range(out.shape[0]):
            out[s] = src[lax.rem(sends[r, base + s] - shift + total, total)]

    put(out_c, 2, me[0] * out_c.shape[0])
    put(out_b, 1, 0)
    put(out_a, 0, 0)


def near_forward_kernel(counts, lrows, lcols, rrows, rslots, me, p0, p1, p2, p3, p4, got_hbm, lv_hbm, rv_hbm,
                        out_ref, src, vals, acc, sems):
    total = out_ref.shape[0]
    cap = rrows.shape[1]
    lcap = lcols.shape[0]
    pieces = (p0, p1, p2, p3, p4)
    part = src.shape[0] - got_hbm.shape[0]
    pairs = pieces_into(pieces + (got_hbm,), src, 0)
    pairs += [(lv_hbm, vals.at[pl.ds(0, lcap)]), (rv_hbm.at[pl.ds(0, cap)], vals.at[pl.ds(lcap, cap)])]
    wait_all(start_all(pairs, sems))
    acc[:total] = src[:total].astype(F32)
    shift = me[0] * total
    forward_tiles(
        counts[0], 0, vals, lambda t: lrows[t],
        lambda t: src[lax.rem(lcols[t] - shift + part, part)], acc,
    )
    forward_tiles(counts[1], lcap, vals, lambda t: rrows[0, t], lambda t: src[part + rslots[0, t]], acc)
    out_ref[...] = acc[:total]


def far_forward_kernel(counts, rrows, rslots, me, p0, p1, p2, p3, p4, got_hbm, rv_hbm, near_hbm, deg_hbm, w_ref,
                       out_ref, src, vals, acc, deg, sems):
    total = out_ref.shape[0]
    cap = rrows.shape[1]
    pieces = (p0, p1, p2, p3, p4)
    pairs = pieces_into((got_hbm,) + pieces, src, 0)
    pairs += [(rv_hbm.at[pl.ds(cap, 2 * cap)], vals), (near_hbm, acc.at[pl.ds(0, total)]), (deg_hbm, deg)]
    wait_all(start_all(pairs, sems))
    forward_tiles(counts[2], 0, vals, lambda t: rrows[1, t], lambda t: src[rslots[1, t]], acc)
    shift = me[0] * p0.shape[0]
    forward_tiles(
        counts[3], cap, vals, lambda t: rrows[2, t],
        lambda t: src[cap + lax.rem(rslots[2, t] - shift + cap, cap)], acc,
    )
    width = deg.shape[2]
    for b in range(total):
        hidden = jnp.concatenate(
            [acc[b, :, k:k + width] / deg[b] for k in range(0, acc.shape[2], width)], axis=1
        ).astype(BF16)
        out_ref[b] = jnp.dot(hidden, w_ref[...], preferred_element_type=F32).astype(BF16)


def body(
    features,
    weight,
    grad_out,
    local_rows,
    local_cols,
    local_values,
    remote_rows,
    remote_slots,
    remote_values,
    send_blocks,
    tile_counts,
):
    rows_dev, width = features.shape
    lcap, rows = local_values.shape[2:4]
    own = rows_dev // rows
    rounds, cap = remote_rows.shape[2:]
    slices = lax.axis_size("feat")
    part = own * slices
    share = cap // slices
    log_nodes = lax.axis_size("node").bit_length() - 1
    bits = [r * log_nodes // rounds for r in range(rounds)]
    tail = (rows, width)

    me = lax.axis_index("feat").astype(jnp.int32).reshape(1)
    counts = tile_counts[0, 0]
    lrows, lcols = local_rows[0, 0], local_cols[0, 0]
    rrows, rslots = remote_rows[0, 0], remote_slots[0, 0]
    sends = send_blocks[0]
    lv = local_values.reshape(lcap, rows, rows)
    rv = remote_values.reshape(rounds * cap, rows, rows)
    feats = features.reshape((own,) + tail)
    go = grad_out.reshape((own,) + tail)

    def blocks(n, kind):
        return jax.ShapeDtypeStruct((n,) + tail, kind)

    def room(n, kind):
        return pltpu.VMEM((n,) + tail, kind)

    def tiles(n, kind=BF16):
        return pltpu.VMEM((n, rows, rows), kind)

    def call(kernel, scalars, specs, args, outs, scratch, flops):
        size = sum(a.size * a.dtype.itemsize for a in args)
        size += sum(o.size * o.dtype.itemsize for o in outs)
        return pl.pallas_call(
            kernel,
            out_shape=tuple(outs),
            in_specs=[SMEM] * len(scalars) + specs,
            out_specs=tuple([VMEM] * len(outs)),
            scratch_shapes=scratch,
            cost_estimate=pl.CostEstimate(flops=flops, bytes_accessed=size, transcendentals=0),
        )(*scalars, *args)

    def sems(n):
        return pltpu.SemaphoreType.DMA((n,))

    tile_flops = 2 * rows * rows * width

    def split_shapes(n):
        return [blocks(n, BF16), blocks(n, BF16), blocks(n // 2, F32), blocks(n // 2, F32), blocks(n, F32)]

    part_feats = spread_out(feats)

    deg, gh, z_right, z_left, z_keep_r, z_keep_l, z_own = call(
        degree_kernel, (counts, lrows, rrows, rslots, me), [ANY, ANY, ANY, VMEM], (lv, rv, go, weight),
        [jax.ShapeDtypeStruct((own, rows, rows), F32), blocks(own, BF16)] + split_shapes(share),
        [tiles(lcap), tiles(rounds * cap), room(own, BF16), tiles(own + 1, F32), room(cap + 1, F32), sems(3)],
        cap * tile_flops,
    )

    def scattered(right, left, keep_r, keep_l):
        a_left = shifted(right, 1)
        a_right = shifted(left, -1)
        h = keep_r.shape[0]
        out_r, out_l = call(
            combine_kernel, (), [VMEM] * 4, (keep_r, keep_l, a_left, a_right),
            [blocks(h, BF16), blocks(h, BF16)], [], 0,
        )
        return a_left, a_right, shifted(out_r, 1), shifted(out_l, -1)

    def finished(own_part, parts):
        return call(finish_kernel, (), [VMEM] * 5, (own_part,) + parts, [blocks(own_part.shape[0], BF16)], [], 0)[0]

    z_parts = scattered(z_right, z_left, z_keep_r, z_keep_l)
    back_a, back_b = call(
        parcels_kernel, (counts, rrows, rslots), [VMEM, VMEM], (rv, gh),
        [blocks(cap, BF16), blocks(cap, BF16)], [room(cap + 1, F32)], 2 * cap * tile_flops,
    )
    got_back_b = swapped(back_b, bits[1])
    got_back_a = swapped(back_a, bits[0])
    got_back_c = swapped(finished(z_own, z_parts), bits[2])

    part_back = call(
        local_back_kernel, (counts, lrows, lcols, me), [VMEM, VMEM], (lv, gh),
        [blocks(part, F32)], [room(part + 1, F32)], lcap * tile_flops,
    )[0]

    need_a, need_b, need_c = call(
        pick_kernel, (sends, me), [ANY] * 5, part_feats,
        [blocks(cap, BF16), blocks(cap, BF16), blocks(share, BF16)], [room(part, BF16), sems(5)], 0,
    )
    got_c = swapped(need_c, bits[2])
    got_b = swapped(need_b, bits[1])
    got_a = swapped(need_a, bits[0])
    far_feats = spread_out(got_c)

    near = call(
        near_forward_kernel, (counts, lrows, lcols, rrows, rslots, me), [ANY] * 8,
        part_feats + (got_a, lv, rv), [blocks(own, F32)],
        [room(part + cap, BF16), tiles(lcap + cap), room(own + 1, F32), sems(8)], (lcap + cap) * tile_flops,
    )[0]

    right, left, keep_r, keep_l, own_part = call(
        merge_kernel, (sends, me), [ANY, VMEM, VMEM, VMEM], (part_back, got_back_a, got_back_b, got_back_c),
        split_shapes(own), [room(part, F32), sems(1)], 0,
    )
    grad_features = finished(own_part, scattered(right, left, keep_r, keep_l))

    output = call(
        far_forward_kernel, (counts, rrows, rslots, me), [ANY] * 9 + [VMEM],
        far_feats + (got_b, rv, near, deg, weight), [blocks(own, BF16)],
        [room(2 * cap, BF16), tiles(2 * cap), room(own + 1, F32), tiles(own, F32), sems(9)],
        2 * cap * tile_flops,
    )[0]
    return (output.reshape(rows_dev, width), grad_features.reshape(rows_dev, width))


def solution(mesh):
    in_specs = (
        P(("node", "feat"), None),
        P(),
        P(("node", "feat"), None),
        P("node", "feat", None),
        P("node", "feat", None),
        P("node", "feat", None, None, None),
        P("node", "feat", None, None),
        P("node", "feat", None, None),
        P("node", "feat", None, None, None, None),
        P("node", None, None),
        P("node", "feat", None),
    )
    out_specs = (P(("node", "feat"), None), P(("node", "feat"), None))
    return jax.shard_map(body, mesh=mesh, in_specs=in_specs, out_specs=out_specs, check_vma=False)
```

```python
import functools

import jax
import jax.numpy as jnp
from jax import lax
from jax.experimental import pallas as pl
from jax.experimental.pallas import tpu as pltpu
from jax.sharding import PartitionSpec as P


UNROLL = 4
F32 = jnp.float32
BF16 = jnp.bfloat16
SMEM = pl.BlockSpec(memory_space=pltpu.SMEM)
VMEM = pl.BlockSpec(memory_space=pltpu.VMEM)
ANY = pl.BlockSpec(memory_space=pl.ANY)
HBM = pl.BlockSpec(memory_space=pltpu.HBM)


def swapped(array, bit):
    return lax.ppermute(array, "node", [(i, i ^ 1 << bit) for i in range(lax.axis_size("node"))])


def shifted(array, step):
    size = lax.axis_size("feat")
    return lax.ppermute(array, "feat", [(i, (i + step) % size) for i in range(size)])


def spread_out(mine):
    half = mine.shape[0] // 2
    before = shifted(mine, 1)
    after = shifted(mine, -1)
    far_low = shifted(before[:half], 1)
    far_high = shifted(after[half:], -1)
    return (mine, after, far_low, far_high, before)


def start_all(pairs, sems):
    copies = [pltpu.make_async_copy(a, b, sems.at[i]) for i, (a, b) in enumerate(pairs)]
    for copy in copies:
        copy.start()
    return copies


def wait_all(copies):
    for copy in copies:
        copy.wait()


def pieces_into(pieces, dst, base):
    pairs = []
    for piece in pieces:
        pairs.append((piece, dst.at[pl.ds(base, piece.shape[0])]))
        base += piece.shape[0]
    return pairs


def for_live(count, step):
    def group(k, carry):
        for u in range(UNROLL):
            t = k * UNROLL + u
            step(t, t < count)
        return carry

    lax.fori_loop(0, pl.cdiv(count, UNROLL), group, 0)


def forward_tiles(count, base, vals, row_of, source_of, acc):
    trash = acc.shape[0] - 1

    def step(t, live):
        row = jnp.where(live, row_of(t), trash)
        acc[row] += jnp.dot(vals[base + t], source_of(t), preferred_element_type=F32)

    for_live(count, step)


def backward_tiles(count, base, vals, row_of, target_of, grads, acc):
    trash = acc.shape[0] - 1

    def step(t, live):
        target = jnp.where(live, target_of(t), trash)
        acc[target] += lax.dot_general(
            vals[base + t], grads[row_of(t)], (((0,), (0,)), ((), ())), preferred_element_type=F32
        )

    for_live(count, step)


def degree_kernel(counts, lrows, rrows, rslots, me, lv_hbm, rv_hbm, go_hbm, w_ref,
                  deg_ref, gh_ref, right_ref, left_ref, keep_r_ref, keep_l_ref, own_ref,
                  lv, rv, go, dacc, acc, sems):
    copies = start_all([(lv_hbm, lv), (rv_hbm, rv), (go_hbm, go)], sems)
    own = deg_ref.shape[0]
    cap = rrows.shape[1]
    dacc[...] = jnp.zeros_like(dacc)
    acc[...] = jnp.zeros_like(acc)
    copies[0].wait()

    def add_rows(vals, base, row_of):
        def step(t, live):
            row = jnp.where(live, row_of(t), own)
            dacc[row] += vals[base + t].astype(F32)

        return step

    for_live(counts[0], add_rows(lv, 0, lambda t: lrows[t]))
    copies[1].wait()
    for r in range(rrows.shape[0]):
        for_live(counts[r + 1], add_rows(rv, r * cap, lambda t: rrows[r, t]))
    copies[2].wait()
    for b in range(own):
        degree = 1.0 + jnp.broadcast_to(jnp.sum(dacc[b], axis=1, keepdims=True), dacc.shape[1:])
        deg_ref[b] = degree
        dense = lax.dot_general(go[b], w_ref[...], (((1,), (1,)), ((), ())), preferred_element_type=F32)
        width = degree.shape[1]
        for k in range(dense.shape[1] // width):
            gh_ref[b, :, k * width:(k + 1) * width] = (
                dense[:, k * width:(k + 1) * width] / degree
            ).astype(BF16)
    last = rrows.shape[0] - 1
    share = own_ref.shape[0]
    shift = me[0] * share
    backward_tiles(
        counts[last + 1], last * cap, rv, lambda t: rrows[last, t],
        lambda t: lax.rem(rslots[last, t] - shift + cap, cap), gh_ref, acc,
    )
    split_out(acc, share, right_ref, left_ref, keep_r_ref, keep_l_ref, own_ref)


def split_out(acc, n, right_ref, left_ref, keep_r_ref, keep_l_ref, own_ref):
    h = n // 2
    right_ref[:h] = acc[2 * n:2 * n + h].astype(BF16)
    right_ref[h:] = acc[n + h:2 * n].astype(BF16)
    left_ref[:h] = acc[2 * n + h:3 * n].astype(BF16)
    left_ref[h:] = acc[3 * n:3 * n + h].astype(BF16)
    keep_r_ref[...] = acc[n:n + h]
    keep_l_ref[...] = acc[3 * n + h:4 * n]
    own_ref[...] = acc[:n]


def parcel_kernel(counts, rows, slots, vals, gh_ref, out, acc, *, r):
    acc[...] = jnp.zeros_like(acc)
    backward_tiles(
        counts[r + 1], 0, vals, lambda t: rows[r, t], lambda t: slots[r, t], gh_ref, acc
    )
    out[...] = acc[:out.shape[0]].astype(BF16)


def local_back_kernel(counts, lrows, lcols, me, lv_ref, gh_ref, out_ref):
    own = gh_ref.shape[0]
    total = out_ref.shape[0] - 1
    out_ref[:own] = gh_ref[...].astype(F32)
    out_ref[own:] = jnp.zeros((total + 1 - own,) + out_ref.shape[1:], F32)
    shift = me[0] * own
    backward_tiles(
        counts[0], 0, lv_ref, lambda t: lrows[t],
        lambda t: lax.rem(lcols[t] - shift + total, total), gh_ref, out_ref,
    )


def combine_kernel(keep_r, keep_l, from_left, from_right, out_r, out_l):
    h = keep_r.shape[0]
    out_r[...] = (keep_r[...] + from_left[:h].astype(F32)).astype(BF16)
    out_l[...] = (keep_l[...] + from_right[:h].astype(F32)).astype(BF16)


def finish_kernel(own, a_left, a_right, b_left, b_right, out):
    h = own.shape[0] // 2
    out[:h] = (own[:h] + a_right[h:].astype(F32) + b_left[...].astype(F32)).astype(BF16)
    out[h:] = (own[h:] + a_left[h:].astype(F32) + b_right[...].astype(F32)).astype(BF16)


def add_arrived(sends, me, gots, own, total, first, count, acc):
    for r, got in enumerate(gots):
        n = got.shape[0]
        base = me[0] * n if r == len(gots) - 1 else 0
        for s in range(n):
            at = lax.rem(sends[r, base + s] - me[0] * own - first + 2 * total, total)

            @pl.when(at < count)
            def _(got=got, s=s, at=at):
                acc[at] += got[s].astype(F32)


def merge_kernel(sends, me, part_hbm, got_a, got_b, got_c, right_ref, left_ref, acc, sems):
    n = right_ref.shape[0]
    h = n // 2
    count = 2 * n
    total = 4 * n
    first = n + h
    wait_all(start_all([(part_hbm.at[pl.ds(first, count)], acc)], sems))
    add_arrived(sends, me, (got_a, got_b, got_c), n, total, first, count, acc)
    right_ref[:h] = acc[h:n].astype(BF16)
    right_ref[h:] = acc[:h].astype(BF16)
    left_ref[:h] = acc[n:n + h].astype(BF16)
    left_ref[h:] = acc[n + h:].astype(BF16)


def rest_kernel(sends, me, part_hbm, got_a, got_b, got_c, keep_r_ref, keep_l_ref, own_ref, acc, sems):
    n = own_ref.shape[0]
    h = n // 2
    total = 4 * n
    first = total - h
    pairs = [
        (part_hbm.at[pl.ds(first, h)], acc.at[pl.ds(0, h)]),
        (part_hbm.at[pl.ds(0, n + h)], acc.at[pl.ds(h, n + h)]),
    ]
    wait_all(start_all(pairs, sems))
    add_arrived(sends, me, (got_a, got_b, got_c), n, total, first, 2 * n, acc)
    keep_l_ref[...] = acc[:h]
    own_ref[...] = acc[h:h + n]
    keep_r_ref[...] = acc[h + n:]


def pick_some(sends, r, base, me, pieces, out, sems):
    own = pieces[0].shape[0]
    total = 4 * own
    count = out.shape[0]

    def begin(s, carry):
        at = lax.rem(sends[r, base + s] - me[0] * own + total, total)
        low = 0
        for piece in pieces:
            size = piece.shape[0]

            @pl.when((at >= low) & (at < low + size))
            def _(piece=piece, low=low):
                pltpu.make_async_copy(piece.at[at - low], out.at[s], sems.at[s]).start()

            low += size
        return carry

    def end(s, carry):
        pltpu.make_async_copy(pieces[0].at[0], out.at[s], sems.at[s]).wait()
        return carry

    lax.fori_loop(0, count, begin, 0)
    return lambda: lax.fori_loop(0, count, end, 0)


def pick_share_kernel(sends, me, p0, p1, p2, p3, p4, out_c, sems):
    pick_some(sends, 2, me[0] * out_c.shape[0], me, (p0, p1, p2, p3, p4), out_c, sems)()


def pick_kernel(sends, me, p0, p1, p2, p3, p4, out_a, out_b, sems_a, sems_b):
    pieces = (p0, p1, p2, p3, p4)
    end_b = pick_some(sends, 1, 0, me, pieces, out_b, sems_b)
    end_a = pick_some(sends, 0, 0, me, pieces, out_a, sems_a)
    end_b()
    end_a()


def near_forward_kernel(counts, lrows, lcols, rrows, rslots, me, p0, p1, p2, p3, p4, got_hbm, lv_hbm, rv_hbm,
                        out_ref, src, vals, acc, sems):
    total = out_ref.shape[0]
    cap = rrows.shape[1]
    lcap = lcols.shape[0]
    pieces = (p0, p1, p2, p3, p4)
    part = src.shape[0] - got_hbm.shape[0]
    pairs = pieces_into(pieces + (got_hbm,), src, 0)
    pairs += [(lv_hbm, vals.at[pl.ds(0, lcap)]), (rv_hbm.at[pl.ds(0, cap)], vals.at[pl.ds(lcap, cap)])]
    wait_all(start_all(pairs, sems))
    acc[:total] = src[:total].astype(F32)
    shift = me[0] * total
    forward_tiles(
        counts[0], 0, vals, lambda t: lrows[t],
        lambda t: src[lax.rem(lcols[t] - shift + part, part)], acc,
    )
    forward_tiles(counts[1], lcap, vals, lambda t: rrows[0, t], lambda t: src[part + rslots[0, t]], acc)
    out_ref[...] = acc[:total]


def far_forward_kernel(counts, rrows, rslots, me, p0, p1, p2, p3, p4, got_hbm, rv_hbm, near_hbm, deg_hbm, w_ref,
                       out_ref, src, vals, acc, deg, sems):
    total = out_ref.shape[0]
    cap = rrows.shape[1]
    pieces = (p0, p1, p2, p3, p4)
    pairs = pieces_into((got_hbm,) + pieces, src, 0)
    pairs += [(rv_hbm.at[pl.ds(cap, 2 * cap)], vals), (near_hbm, acc.at[pl.ds(0, total)]), (deg_hbm, deg)]
    wait_all(start_all(pairs, sems))
    forward_tiles(counts[2], 0, vals, lambda t: rrows[1, t], lambda t: src[rslots[1, t]], acc)
    shift = me[0] * p0.shape[0]
    forward_tiles(
        counts[3], cap, vals, lambda t: rrows[2, t],
        lambda t: src[cap + lax.rem(rslots[2, t] - shift + cap, cap)], acc,
    )
    width = deg.shape[2]
    for b in range(total):
        hidden = jnp.concatenate(
            [acc[b, :, k:k + width] / deg[b] for k in range(0, acc.shape[2], width)], axis=1
        ).astype(BF16)
        out_ref[b] = jnp.dot(hidden, w_ref[...], preferred_element_type=F32).astype(BF16)


def body(
    features,
    weight,
    grad_out,
    local_rows,
    local_cols,
    local_values,
    remote_rows,
    remote_slots,
    remote_values,
    send_blocks,
    tile_counts,
):
    rows_dev, width = features.shape
    lcap, rows = local_values.shape[2:4]
    own = rows_dev // rows
    rounds, cap = remote_rows.shape[2:]
    slices = lax.axis_size("feat")
    part = own * slices
    share = cap // slices
    log_nodes = lax.axis_size("node").bit_length() - 1
    bits = [r * log_nodes // rounds for r in range(rounds)]
    tail = (rows, width)

    me = lax.axis_index("feat").astype(jnp.int32).reshape(1)
    counts = tile_counts[0, 0]
    lrows, lcols = local_rows[0, 0], local_cols[0, 0]
    rrows, rslots = remote_rows[0, 0], remote_slots[0, 0]
    sends = send_blocks[0]
    lv = local_values.reshape(lcap, rows, rows)
    rv = remote_values.reshape(rounds * cap, rows, rows)
    feats = features.reshape((own,) + tail)
    go = grad_out.reshape((own,) + tail)

    def blocks(n, kind):
        return jax.ShapeDtypeStruct((n,) + tail, kind)

    def room(n, kind):
        return pltpu.VMEM((n,) + tail, kind)

    def tiles(n, kind=BF16):
        return pltpu.VMEM((n, rows, rows), kind)

    def call(kernel, scalars, specs, args, outs, scratch, flops):
        size = sum(a.size * a.dtype.itemsize for a in args)
        size += sum(o.size * o.dtype.itemsize for o in outs)
        return pl.pallas_call(
            kernel,
            out_shape=tuple(outs),
            in_specs=[SMEM] * len(scalars) + specs,
            out_specs=tuple([VMEM] * len(outs)),
            scratch_shapes=scratch,
            cost_estimate=pl.CostEstimate(flops=flops, bytes_accessed=size, transcendentals=0),
        )(*scalars, *args)

    def sems(n):
        return pltpu.SemaphoreType.DMA((n,))

    tile_flops = 2 * rows * rows * width

    def split_shapes(n):
        return [blocks(n, BF16), blocks(n, BF16), blocks(n // 2, F32), blocks(n // 2, F32), blocks(n, F32)]

    def first_round(right, left):
        return shifted(right, 1), shifted(left, -1)

    def second_round(a_left, a_right, keep_r, keep_l):
        h = keep_r.shape[0]
        out_r, out_l = call(
            combine_kernel, (), [VMEM] * 4, (keep_r, keep_l, a_left, a_right),
            [blocks(h, BF16), blocks(h, BF16)], [], 0,
        )
        return shifted(out_r, 1), shifted(out_l, -1)

    def finished(own_part, parts):
        return call(finish_kernel, (), [VMEM] * 5, (own_part,) + parts, [blocks(own_part.shape[0], BF16)], [], 0)[0]

    part_feats = spread_out(feats)

    deg, gh, z_right, z_left, z_keep_r, z_keep_l, z_own = call(
        degree_kernel, (counts, lrows, rrows, rslots, me), [ANY, ANY, ANY, VMEM], (lv, rv, go, weight),
        [jax.ShapeDtypeStruct((own, rows, rows), F32), blocks(own, BF16)] + split_shapes(share),
        [tiles(lcap), tiles(rounds * cap), room(own, BF16), tiles(own + 1, F32), room(cap + 1, F32), sems(3)],
        cap * tile_flops,
    )
    z_first = first_round(z_right, z_left)

    def parcel(r):
        return pl.pallas_call(
            functools.partial(parcel_kernel, r=r),
            out_shape=blocks(cap, BF16),
            grid=(1,),
            in_specs=[SMEM] * 3 + [
                pl.BlockSpec((cap, rows, rows), lambda i: (r, 0, 0)),
                pl.BlockSpec((own,) + tail, lambda i: (0, 0, 0)),
            ],
            out_specs=pl.BlockSpec((cap,) + tail, lambda i: (0, 0, 0)),
            scratch_shapes=[room(cap + 1, F32)],
            cost_estimate=pl.CostEstimate(
                flops=cap * tile_flops, bytes_accessed=2 * cap * rows * (rows + width), transcendentals=0
            ),
        )(counts, rrows, rslots, rv, gh)

    got_back_b = swapped(parcel(1), bits[1])
    got_back_a = swapped(parcel(0), bits[0])
    z_parts = z_first + second_round(*z_first, z_keep_r, z_keep_l)
    got_back_c = swapped(finished(z_own, z_parts), bits[2])

    part_back = call(
        local_back_kernel, (counts, lrows, lcols, me), [VMEM, VMEM], (lv, gh),
        [blocks(part + 1, F32)], [], lcap * tile_flops,
    )[0]

    need_c = call(pick_share_kernel, (sends, me), [HBM] * 5, part_feats, [blocks(share, BF16)], [sems(share)], 0)[0]
    got_c = swapped(need_c, bits[2])
    need_a, need_b = call(
        pick_kernel, (sends, me), [HBM] * 5, part_feats,
        [blocks(cap, BF16), blocks(cap, BF16)], [sems(cap), sems(cap)], 0,
    )
    got_b = swapped(need_b, bits[1])
    got_a = swapped(need_a, bits[0])
    far_feats = spread_out(got_c)

    near = call(
        near_forward_kernel, (counts, lrows, lcols, rrows, rslots, me), [HBM] * 6 + [ANY] * 2,
        part_feats + (got_a, lv, rv), [blocks(own, F32)],
        [room(part + cap, BF16), tiles(lcap + cap), room(own + 1, F32), sems(8)], (lcap + cap) * tile_flops,
    )[0]

    arrived = (part_back, got_back_a, got_back_b, got_back_c)
    right, left = call(
        merge_kernel, (sends, me), [ANY, VMEM, VMEM, VMEM], arrived,
        [blocks(own, BF16), blocks(own, BF16)], [room(2 * own, F32), sems(1)], 0,
    )
    first = first_round(right, left)
    keep_r, keep_l, own_part = call(
        rest_kernel, (sends, me), [ANY, VMEM, VMEM, VMEM], arrived,
        [blocks(own // 2, F32), blocks(own // 2, F32), blocks(own, F32)], [room(2 * own, F32), sems(2)], 0,
    )
    grad_features = finished(own_part, first + second_round(*first, keep_r, keep_l))

    output = call(
        far_forward_kernel, (counts, rrows, rslots, me), [HBM] * 6 + [ANY] * 3 + [VMEM],
        far_feats + (got_b, rv, near, deg, weight), [blocks(own, BF16)],
        [room(2 * cap, BF16), tiles(2 * cap), room(own + 1, F32), tiles(own, F32), sems(9)],
        2 * cap * tile_flops,
    )[0]
    return (output.reshape(rows_dev, width), grad_features.reshape(rows_dev, width))


def solution(mesh):
    in_specs = (
        P(("node", "feat"), None),
        P(),
        P(("node", "feat"), None),
        P("node", "feat", None),
        P("node", "feat", None),
        P("node", "feat", None, None, None),
        P("node", "feat", None, None),
        P("node", "feat", None, None),
        P("node", "feat", None, None, None, None),
        P("node", None, None),
        P("node", "feat", None),
    )
    out_specs = (P(("node", "feat"), None), P(("node", "feat"), None))
    return jax.shard_map(body, mesh=mesh, in_specs=in_specs, out_specs=out_specs, check_vma=False)
```

```python
import jax
import jax.numpy as jnp
from jax import lax
from jax.experimental import pallas as pl
from jax.experimental.pallas import tpu as pltpu
from jax.sharding import PartitionSpec as P


UNROLL = 4
F32 = jnp.float32
BF16 = jnp.bfloat16
SMEM = pl.BlockSpec(memory_space=pltpu.SMEM)
VMEM = pl.BlockSpec(memory_space=pltpu.VMEM)
ANY = pl.BlockSpec(memory_space=pl.ANY)


def swapped(array, bit):
    return lax.ppermute(array, "node", [(i, i ^ 1 << bit) for i in range(lax.axis_size("node"))])


def shifted(array, step):
    size = lax.axis_size("feat")
    return lax.ppermute(array, "feat", [(i, (i + step) % size) for i in range(size)])


def spread_relayed(mine):
    half = mine.shape[0] // 2
    before = shifted(mine, 1)
    after = shifted(mine, -1)
    far_low = shifted(before[:half], 1)
    far_high = shifted(after[half:], -1)
    return (mine, after, far_low, far_high, before)


def spread_direct(mine):
    before = shifted(mine, 1)
    after = shifted(mine, -1)
    far = shifted(mine, 2)
    return (mine, after, far, before)


def scattered(to_next, to_far, to_before):
    return shifted(to_next, 1), shifted(to_far, 2), shifted(to_before, -1)


def start_all(pairs, sems):
    copies = [pltpu.make_async_copy(a, b, sems.at[i]) for i, (a, b) in enumerate(pairs)]
    for copy in copies:
        copy.start()
    return copies


def wait_all(copies):
    for copy in copies:
        copy.wait()


def pieces_into(pieces, dst, base):
    pairs = []
    for piece in pieces:
        pairs.append((piece, dst.at[pl.ds(base, piece.shape[0])]))
        base += piece.shape[0]
    return pairs


def for_live(count, step):
    def group(k, carry):
        for u in range(UNROLL):
            t = k * UNROLL + u
            step(t, t < count)
        return carry

    lax.fori_loop(0, pl.cdiv(count, UNROLL), group, 0)


def forward_tiles(count, base, vals, row_of, source_of, acc):
    trash = acc.shape[0] - 1

    def step(t, live):
        row = jnp.where(live, row_of(t), trash)
        acc[row] += jnp.dot(vals[base + t], source_of(t), preferred_element_type=F32)

    for_live(count, step)


def backward_tiles(count, base, vals, row_of, target_of, grads, acc):
    trash = acc.shape[0] - 1

    def step(t, live):
        target = jnp.where(live, target_of(t), trash)
        acc[target] += lax.dot_general(
            vals[base + t], grads[row_of(t)], (((0,), (0,)), ((), ())), preferred_element_type=F32
        )

    for_live(count, step)


def degree_kernel(counts, lrows, rrows, rslots, me, lv_hbm, rv_hbm, go_hbm, w_ref,
                  deg_ref, gh_ref, next_ref, far_ref, before_ref, own_ref, out_b, out_a,
                  lv, rv, go, dacc, acc, sems):
    copies = start_all([(lv_hbm, lv), (rv_hbm, rv), (go_hbm, go)], sems)
    own = deg_ref.shape[0]
    cap = rrows.shape[1]
    dacc[...] = jnp.zeros_like(dacc)
    acc[...] = jnp.zeros_like(acc)
    copies[0].wait()

    def add_rows(vals, base, row_of):
        def step(t, live):
            row = jnp.where(live, row_of(t), own)
            dacc[row] += vals[base + t].astype(F32)

        return step

    for_live(counts[0], add_rows(lv, 0, lambda t: lrows[t]))
    copies[1].wait()
    for r in range(rrows.shape[0]):
        for_live(counts[r + 1], add_rows(rv, r * cap, lambda t: rrows[r, t]))
    copies[2].wait()
    for b in range(own):
        degree = 1.0 + jnp.broadcast_to(jnp.sum(dacc[b], axis=1, keepdims=True), dacc.shape[1:])
        deg_ref[b] = degree
        dense = lax.dot_general(go[b], w_ref[...], (((1,), (1,)), ((), ())), preferred_element_type=F32)
        width = degree.shape[1]
        for k in range(dense.shape[1] // width):
            gh_ref[b, :, k * width:(k + 1) * width] = (
                dense[:, k * width:(k + 1) * width] / degree
            ).astype(BF16)
    share = own_ref.shape[0]
    shift = me[0] * share
    backward_tiles(
        counts[3], 2 * cap, rv, lambda t: rrows[2, t],
        lambda t: lax.rem(rslots[2, t] - shift + cap, cap), gh_ref, acc,
    )
    split_out(acc, share, next_ref, far_ref, before_ref, own_ref)
    for r, out in ((1, out_b), (0, out_a)):
        acc[...] = jnp.zeros_like(acc)
        backward_tiles(
            counts[r + 1], r * cap, rv, lambda t: rrows[r, t], lambda t: rslots[r, t], gh_ref, acc
        )
        out[...] = acc[:cap].astype(BF16)


def split_out(acc, n, next_ref, far_ref, before_ref, own_ref):
    next_ref[...] = acc[n:2 * n].astype(BF16)
    far_ref[...] = acc[2 * n:3 * n].astype(BF16)
    before_ref[...] = acc[3 * n:4 * n].astype(BF16)
    own_ref[...] = acc[:n]


def merge_kernel(counts, lrows, lcols, sends, me, lv_hbm, gh_hbm, a_hbm, b_hbm, c_hbm,
                 next_ref, far_ref, before_ref, own_ref, lv, gh, got_a, got_b, got_c, acc, sems):
    copies = start_all([(lv_hbm, lv), (gh_hbm, gh), (a_hbm, got_a), (b_hbm, got_b), (c_hbm, got_c)], sems)
    own = gh.shape[0]
    total = acc.shape[0] - 1
    acc[own:] = jnp.zeros((total + 1 - own,) + acc.shape[1:], F32)
    wait_all(copies[:2])
    acc[:own] = gh[...].astype(F32)
    shift = me[0] * own
    backward_tiles(
        counts[0], 0, lv, lambda t: lrows[t],
        lambda t: lax.rem(lcols[t] - shift + total, total), gh, acc,
    )
    wait_all(copies[2:])
    for r, (got, base) in enumerate(((got_a, 0), (got_b, 0), (got_c, me[0] * got_c.shape[0]))):
        for s in range(got.shape[0]):
            acc[lax.rem(sends[r, base + s] - shift + total, total)] += got[s].astype(F32)
    split_out(acc, own, next_ref, far_ref, before_ref, own_ref)


def finish_kernel(own, a, b, c, out):
    out[...] = (own[...] + a[...].astype(F32) + b[...].astype(F32) + c[...].astype(F32)).astype(BF16)


def feat_kernel(counts, lrows, lcols, sends, me, p0, p1, p2, p3, p4, lv_hbm, out_a, out_b, out_c, near_ref,
                src, lv, acc, sems, sems_a, sems_b, sems_c):
    copies = start_all(pieces_into((p0, p1, p2, p3, p4), src, 0) + [(lv_hbm, lv)], sems)
    total = src.shape[0]
    own = near_ref.shape[0]
    shift = me[0] * own
    wait_all(copies[:5])
    picks = (
        (out_c, 2, me[0] * out_c.shape[0], sems_c), (out_b, 1, 0, sems_b), (out_a, 0, 0, sems_a)
    )

    def begin(out, r, base, marks):
        def one(s, carry):
            at = lax.rem(sends[r, base + s] - shift + total, total)
            pltpu.make_async_copy(src.at[at], out.at[s], marks.at[s]).start()
            return carry

        lax.fori_loop(0, out.shape[0], one, 0)

    def end(out, r, base, marks):
        def one(s, carry):
            pltpu.make_async_copy(src.at[0], out.at[s], marks.at[s]).wait()
            return carry

        lax.fori_loop(0, out.shape[0], one, 0)

    for pick in picks:
        begin(*pick)
    acc[:own] = src[:own].astype(F32)
    copies[5].wait()
    forward_tiles(
        counts[0], 0, lv, lambda t: lrows[t], lambda t: src[lax.rem(lcols[t] - shift + total, total)], acc
    )
    near_ref[...] = acc[:own]
    for pick in picks:
        end(*pick)


def far_kernel(counts, rrows, rslots, me, a_hbm, b_hbm, p0, p1, p2, p3, rv_hbm, near_hbm, deg_hbm, w_ref,
               out_ref, src, vals, acc, deg, sems):
    total = out_ref.shape[0]
    cap = rrows.shape[1]
    pairs = [(near_hbm, acc.at[pl.ds(0, total)]), (rv_hbm, vals)]
    pairs += pieces_into((a_hbm, b_hbm, p0, p1, p2, p3), src, 0) + [(deg_hbm, deg)]
    wait_all(start_all(pairs, sems))
    for r in range(2):
        forward_tiles(
            counts[r + 1], r * cap, vals, lambda t: rrows[r, t], lambda t: src[r * cap + rslots[r, t]], acc
        )
    shift = me[0] * p0.shape[0]
    forward_tiles(
        counts[3], 2 * cap, vals, lambda t: rrows[2, t],
        lambda t: src[2 * cap + lax.rem(rslots[2, t] - shift + cap, cap)], acc,
    )
    width = deg.shape[2]
    for b in range(total):
        hidden = jnp.concatenate(
            [acc[b, :, k:k + width] / deg[b] for k in range(0, acc.shape[2], width)], axis=1
        ).astype(BF16)
        out_ref[b] = jnp.dot(hidden, w_ref[...], preferred_element_type=F32).astype(BF16)


def body(
    features,
    weight,
    grad_out,
    local_rows,
    local_cols,
    local_values,
    remote_rows,
    remote_slots,
    remote_values,
    send_blocks,
    tile_counts,
):
    rows_dev, width = features.shape
    lcap, rows = local_values.shape[2:4]
    own = rows_dev // rows
    rounds, cap = remote_rows.shape[2:]
    slices = lax.axis_size("feat")
    part = own * slices
    share = cap // slices
    log_nodes = lax.axis_size("node").bit_length() - 1
    bits = [r * log_nodes // rounds for r in range(rounds)]
    tail = (rows, width)

    me = lax.axis_index("feat").astype(jnp.int32).reshape(1)
    counts = tile_counts[0, 0]
    lrows, lcols = local_rows[0, 0], local_cols[0, 0]
    rrows, rslots = remote_rows[0, 0], remote_slots[0, 0]
    sends = send_blocks[0]
    lv = local_values.reshape(lcap, rows, rows)
    rv = remote_values.reshape(rounds * cap, rows, rows)
    feats = features.reshape((own,) + tail)
    go = grad_out.reshape((own,) + tail)

    def blocks(n, kind):
        return jax.ShapeDtypeStruct((n,) + tail, kind)

    def room(n, kind):
        return pltpu.VMEM((n,) + tail, kind)

    def tiles(n, kind=BF16):
        return pltpu.VMEM((n, rows, rows), kind)

    def call(kernel, scalars, args, outs, scratch, flops, in_place=(), out_place=()):
        size = sum(a.size * a.dtype.itemsize for a in args)
        size += sum(o.size * o.dtype.itemsize for o in outs)
        return pl.pallas_call(
            kernel,
            out_shape=tuple(outs),
            in_specs=[SMEM] * len(scalars) + [VMEM if i in in_place else ANY for i in range(len(args))],
            out_specs=tuple(ANY if i in out_place else VMEM for i in range(len(outs))),
            scratch_shapes=scratch,
            cost_estimate=pl.CostEstimate(flops=flops, bytes_accessed=size, transcendentals=0),
        )(*scalars, *args)

    def sems(n):
        return pltpu.SemaphoreType.DMA((n,))

    tile_flops = 2 * rows * rows * width

    def split_shapes(n):
        return [blocks(n, BF16), blocks(n, BF16), blocks(n, BF16), blocks(n, F32)]

    def finished(own_part, arrived):
        n = own_part.shape[0]
        return call(finish_kernel, (), (own_part,) + arrived, [blocks(n, BF16)], [], 0, range(4))[0]

    part_feats = spread_relayed(feats)

    deg, gh, z_next, z_far, z_before, z_own, back_b, back_a = call(
        degree_kernel, (counts, lrows, rrows, rslots, me), (lv, rv, go, weight),
        [jax.ShapeDtypeStruct((own, rows, rows), F32), blocks(own, BF16)] + split_shapes(share)
        + [blocks(cap, BF16), blocks(cap, BF16)],
        [tiles(lcap), tiles(rounds * cap), room(own, BF16), tiles(own + 1, F32), room(cap + 1, F32), sems(3)],
        rounds * cap * tile_flops, (3,),
    )
    z_arrived = scattered(z_next, z_far, z_before)
    got_back_b = swapped(back_b, bits[1])
    got_back_a = swapped(back_a, bits[0])
    got_back_c = swapped(finished(z_own, z_arrived), bits[2])

    need_a, need_b, need_c, near = call(
        feat_kernel, (counts, lrows, lcols, sends, me), part_feats + (lv,),
        [blocks(cap, BF16), blocks(cap, BF16), blocks(share, BF16), blocks(own, F32)],
        [room(part, BF16), tiles(lcap), room(own + 1, F32), sems(6), sems(cap), sems(cap), sems(share)],
        lcap * tile_flops, (), range(3),
    )
    got_c = swapped(need_c, bits[2])
    got_b = swapped(need_b, bits[1])
    got_a = swapped(need_a, bits[0])

    to_next, to_far, to_before, own_part = call(
        merge_kernel, (counts, lrows, lcols, sends, me), (lv, gh, got_back_a, got_back_b, got_back_c),
        split_shapes(own),
        [tiles(lcap), room(own, BF16), room(cap, BF16), room(cap, BF16), room(share, BF16), room(part + 1, F32), sems(5)],
        lcap * tile_flops,
    )
    grad_features = finished(own_part, scattered(to_next, to_far, to_before))

    output = call(
        far_kernel, (counts, rrows, rslots, me),
        (got_a, got_b) + spread_direct(got_c) + (rv, near, deg, weight), [blocks(own, BF16)],
        [room(rounds * cap, BF16), tiles(rounds * cap), room(own + 1, F32), tiles(own, F32), sems(9)],
        rounds * cap * tile_flops, (9,),
    )[0]
    return (output.reshape(rows_dev, width), grad_features.reshape(rows_dev, width))


def solution(mesh):
    in_specs = (
        P(("node", "feat"), None),
        P(),
        P(("node", "feat"), None),
        P("node", "feat", None),
        P("node", "feat", None),
        P("node", "feat", None, None, None),
        P("node", "feat", None, None),
        P("node", "feat", None, None),
        P("node", "feat", None, None, None, None),
        P("node", None, None),
        P("node", "feat", None),
    )
    out_specs = (P(("node", "feat"), None), P(("node", "feat"), None))
    return jax.shard_map(body, mesh=mesh, in_specs=in_specs, out_specs=out_specs, check_vma=False)
```

```python
import jax
import jax.numpy as jnp
from jax import lax
from jax.experimental import pallas as pl
from jax.experimental.pallas import tpu as pltpu
from jax.sharding import PartitionSpec as P


UNROLL = 4
F32 = jnp.float32
BF16 = jnp.bfloat16
SMEM = pl.BlockSpec(memory_space=pltpu.SMEM)
VMEM = pl.BlockSpec(memory_space=pltpu.VMEM)
ANY = pl.BlockSpec(memory_space=pl.ANY)


def swapped(array, bit):
    return lax.ppermute(array, "node", [(i, i ^ 1 << bit) for i in range(lax.axis_size("node"))])


def shifted(array, step):
    size = lax.axis_size("feat")
    return lax.ppermute(array, "feat", [(i, (i + step) % size) for i in range(size)])


def spread_relayed(mine):
    half = mine.shape[0] // 2
    before = shifted(mine, 1)
    after = shifted(mine, -1)
    far_low = shifted(before[:half], 1)
    far_high = shifted(after[half:], -1)
    return (mine, after, far_low, far_high, before)


def spread_direct(mine):
    before = shifted(mine, 1)
    after = shifted(mine, -1)
    far = shifted(mine, 2)
    return (mine, after, far, before)


def scattered(to_next, to_far, to_before):
    return shifted(to_next, 1), shifted(to_far, 2), shifted(to_before, -1)


def start_all(pairs, sems):
    copies = [pltpu.make_async_copy(a, b, sems.at[i]) for i, (a, b) in enumerate(pairs)]
    for copy in copies:
        copy.start()
    return copies


def wait_all(copies):
    for copy in copies:
        copy.wait()


def pieces_into(pieces, dst, base):
    pairs = []
    for piece in pieces:
        pairs.append((piece, dst.at[pl.ds(base, piece.shape[0])]))
        base += piece.shape[0]
    return pairs


def for_live(count, step):
    def group(k, carry):
        for u in range(UNROLL):
            t = k * UNROLL + u
            step(t, t < count)
        return carry

    lax.fori_loop(0, pl.cdiv(count, UNROLL), group, 0)


def forward_tiles(count, base, vals, row_of, source_of, acc):
    trash = acc.shape[0] - 1

    def step(t, live):
        row = jnp.where(live, row_of(t), trash)
        acc[row] += jnp.dot(vals[base + t], source_of(t), preferred_element_type=F32)

    for_live(count, step)


def backward_tiles(count, base, vals, row_of, target_of, grads, acc):
    trash = acc.shape[0] - 1

    def step(t, live):
        target = jnp.where(live, target_of(t), trash)
        acc[target] += lax.dot_general(
            vals[base + t], grads[row_of(t)], (((0,), (0,)), ((), ())), preferred_element_type=F32
        )

    for_live(count, step)


def degree_kernel(counts, lrows, rrows, rslots, me, lv_hbm, rv_hbm, go_hbm, w_ref,
                  deg_ref, gh_ref, next_ref, far_ref, before_ref, own_ref, out_b, out_a,
                  lv, rv, go, dacc, acc, sems):
    copies = start_all([(lv_hbm, lv), (rv_hbm, rv), (go_hbm, go)], sems)
    own = deg_ref.shape[0]
    cap = rrows.shape[2]
    dacc[...] = jnp.zeros_like(dacc)
    acc[...] = jnp.zeros_like(acc)
    copies[0].wait()

    def add_rows(vals, base, row_of):
        def step(t, live):
            row = jnp.where(live, row_of(t), own)
            dacc[row] += vals[base + t].astype(F32)

        return step

    for_live(counts[0], add_rows(lv, 0, lambda t: lrows[t]))
    copies[1].wait()
    for r in range(rrows.shape[0]):
        for_live(counts[r + 1], add_rows(rv, r * cap, lambda t: rrows[r, 0, t]))
    copies[2].wait()
    for b in range(own):
        degree = 1.0 + jnp.broadcast_to(jnp.sum(dacc[b], axis=1, keepdims=True), dacc.shape[1:])
        deg_ref[b] = degree
        dense = lax.dot_general(go[b], w_ref[...], (((1,), (1,)), ((), ())), preferred_element_type=F32)
        width = degree.shape[1]
        for k in range(dense.shape[1] // width):
            gh_ref[b, :, k * width:(k + 1) * width] = (
                dense[:, k * width:(k + 1) * width] / degree
            ).astype(BF16)
    share = own_ref.shape[0]
    shift = me[0] * share
    backward_tiles(
        counts[3], 2 * cap, rv, lambda t: rrows[2, 0, t],
        lambda t: lax.rem(rslots[2, 0, t] - shift + cap, cap), gh_ref, acc,
    )
    split_out(acc, share, next_ref, far_ref, before_ref, own_ref)
    for r, out in ((1, out_b), (0, out_a)):
        acc[...] = jnp.zeros_like(acc)
        backward_tiles(
            counts[r + 1], r * cap, rv, lambda t: rrows[r, 0, t], lambda t: rslots[r, 0, t], gh_ref, acc
        )
        out[...] = acc[:cap].astype(BF16)


def split_out(acc, n, next_ref, far_ref, before_ref, own_ref):
    next_ref[...] = acc[n:2 * n].astype(BF16)
    far_ref[...] = acc[2 * n:3 * n].astype(BF16)
    before_ref[...] = acc[3 * n:4 * n].astype(BF16)
    own_ref[...] = acc[:n]


def merge_kernel(counts, lrows, lcols, sends, me, lv_hbm, gh_hbm, a_hbm, b_hbm, c_hbm,
                 right_ref, left_ref, keep_r_ref, keep_l_ref, own_ref, lv, gh, got_a, got_b, got_c, acc, sems):
    copies = start_all([(lv_hbm, lv), (gh_hbm, gh), (a_hbm, got_a), (b_hbm, got_b), (c_hbm, got_c)], sems)
    own = gh.shape[0]
    total = acc.shape[0] - 1
    acc[own:] = jnp.zeros((total + 1 - own,) + acc.shape[1:], F32)
    wait_all(copies[:2])
    acc[:own] = gh[...].astype(F32)
    shift = me[0] * own
    backward_tiles(
        counts[0], 0, lv, lambda t: lrows[t],
        lambda t: lax.rem(lcols[t] - shift + total, total), gh, acc,
    )
    wait_all(copies[2:])
    for r, (got, base) in enumerate(((got_a, 0), (got_b, 0), (got_c, me[0] * got_c.shape[0]))):
        for s in range(got.shape[0]):
            acc[lax.rem(sends[r, 0, base + s] - shift + total, total)] += got[s].astype(F32)
    n, h = own, own // 2
    right_ref[:h] = acc[2 * n:2 * n + h].astype(BF16)
    right_ref[h:] = acc[n + h:2 * n].astype(BF16)
    left_ref[:h] = acc[2 * n + h:3 * n].astype(BF16)
    left_ref[h:] = acc[3 * n:3 * n + h].astype(BF16)
    keep_r_ref[...] = acc[n:n + h]
    keep_l_ref[...] = acc[3 * n + h:4 * n]
    own_ref[...] = acc[:n]


def combine_kernel(keep_r, keep_l, from_left, from_right, out_r, out_l):
    out_r[...] = (keep_r[...] + from_left[...].astype(F32)).astype(BF16)
    out_l[...] = (keep_l[...] + from_right[...].astype(F32)).astype(BF16)


def relay_finish_kernel(own, a_left, a_right, b_left, b_right, out):
    h = own.shape[0] // 2
    out[:h] = (own[:h] + a_right[...].astype(F32) + b_left[...].astype(F32)).astype(BF16)
    out[h:] = (own[h:] + a_left[...].astype(F32) + b_right[...].astype(F32)).astype(BF16)


def finish_kernel(own, a, b, c, out):
    out[...] = (own[...] + a[...].astype(F32) + b[...].astype(F32) + c[...].astype(F32)).astype(BF16)


def feat_kernel(counts, lrows, lcols, sends, me, p0, p1, p2, p3, p4, lv_hbm, out_a, out_b, out_c, near_ref,
                src, lv, acc, sems, sems_a, sems_b, sems_c):
    copies = start_all(pieces_into((p0, p1, p2, p3, p4), src, 0) + [(lv_hbm, lv)], sems)
    total = src.shape[0]
    own = near_ref.shape[0]
    shift = me[0] * own
    wait_all(copies[:5])
    picks = (
        (out_c, 2, me[0] * out_c.shape[0], sems_c), (out_b, 1, 0, sems_b), (out_a, 0, 0, sems_a)
    )

    def begin(out, r, base, marks):
        def one(s, carry):
            at = lax.rem(sends[r, 0, base + s] - shift + total, total)
            pltpu.make_async_copy(src.at[at], out.at[s], marks.at[s]).start()
            return carry

        lax.fori_loop(0, out.shape[0], one, 0)

    def end(out, r, base, marks):
        def one(s, carry):
            pltpu.make_async_copy(src.at[0], out.at[s], marks.at[s]).wait()
            return carry

        lax.fori_loop(0, out.shape[0], one, 0)

    for pick in picks:
        begin(*pick)
    acc[:own] = src[:own].astype(F32)
    copies[5].wait()
    forward_tiles(
        counts[0], 0, lv, lambda t: lrows[t], lambda t: src[lax.rem(lcols[t] - shift + total, total)], acc
    )
    near_ref[...] = acc[:own]
    for pick in picks:
        end(*pick)


def far_kernel(counts, rrows, rslots, me, a_hbm, b_hbm, p0, p1, p2, p3, rv_hbm, near_hbm, deg_hbm, w_ref,
               out_ref, src, vals, acc, deg, sems):
    total = out_ref.shape[0]
    cap = rrows.shape[2]
    pairs = [(near_hbm, acc.at[pl.ds(0, total)]), (rv_hbm, vals)]
    pairs += pieces_into((a_hbm, b_hbm, p0, p1, p2, p3), src, 0) + [(deg_hbm, deg)]
    wait_all(start_all(pairs, sems))
    for r in range(2):
        forward_tiles(
            counts[r + 1], r * cap, vals, lambda t: rrows[r, 0, t], lambda t: src[r * cap + rslots[r, 0, t]], acc
        )
    shift = me[0] * p0.shape[0]
    forward_tiles(
        counts[3], 2 * cap, vals, lambda t: rrows[2, 0, t],
        lambda t: src[2 * cap + lax.rem(rslots[2, 0, t] - shift + cap, cap)], acc,
    )
    width = deg.shape[2]
    for b in range(total):
        hidden = jnp.concatenate(
            [acc[b, :, k:k + width] / deg[b] for k in range(0, acc.shape[2], width)], axis=1
        ).astype(BF16)
        out_ref[b] = jnp.dot(hidden, w_ref[...], preferred_element_type=F32).astype(BF16)


def body(
    features,
    weight,
    grad_out,
    local_rows,
    local_cols,
    local_values,
    remote_rows,
    remote_slots,
    remote_values,
    send_blocks,
    tile_counts,
):
    rows_dev, width = features.shape
    lcap, rows = local_values.shape[2:4]
    own = rows_dev // rows
    rounds, cap = remote_rows.shape[2:]
    slices = lax.axis_size("feat")
    part = own * slices
    share = cap // slices
    half = own // 2
    log_nodes = lax.axis_size("node").bit_length() - 1
    bits = [r * log_nodes // rounds for r in range(rounds)]
    tail = (rows, width)

    me = lax.axis_index("feat").astype(jnp.int32).reshape(1)
    counts = tile_counts[0, 0]
    lrows, lcols = local_rows[0, 0], local_cols[0, 0]
    rrows, rslots, sends = (a.reshape(rounds, 1, cap) for a in (remote_rows, remote_slots, send_blocks))
    lv = local_values.reshape(lcap, rows, rows)
    rv = remote_values.reshape(rounds * cap, rows, rows)
    feats = features.reshape((own,) + tail)
    go = grad_out.reshape((own,) + tail)

    def blocks(n, kind):
        return jax.ShapeDtypeStruct((n,) + tail, kind)

    def room(n, kind):
        return pltpu.VMEM((n,) + tail, kind)

    def tiles(n, kind=BF16):
        return pltpu.VMEM((n, rows, rows), kind)

    def call(kernel, scalars, args, outs, scratch, flops, in_place=(), out_place=()):
        size = sum(a.size * a.dtype.itemsize for a in args)
        size += sum(o.size * o.dtype.itemsize for o in outs)
        return pl.pallas_call(
            kernel,
            out_shape=tuple(outs),
            in_specs=[SMEM] * len(scalars) + [VMEM if i in in_place else ANY for i in range(len(args))],
            out_specs=tuple(ANY if i in out_place else VMEM for i in range(len(outs))),
            scratch_shapes=scratch,
            cost_estimate=pl.CostEstimate(flops=flops, bytes_accessed=size, transcendentals=0),
        )(*scalars, *args)

    def sems(n):
        return pltpu.SemaphoreType.DMA((n,))

    tile_flops = 2 * rows * rows * width

    def split_shapes(n):
        return [blocks(n, BF16), blocks(n, BF16), blocks(n, BF16), blocks(n, F32)]

    def finished(own_part, arrived):
        n = own_part.shape[0]
        return call(finish_kernel, (), (own_part,) + arrived, [blocks(n, BF16)], [], 0, range(4))[0]

    part_feats = spread_relayed(feats)

    deg, gh, z_next, z_far, z_before, z_own, back_b, back_a = call(
        degree_kernel, (counts, lrows, rrows, rslots, me), (lv, rv, go, weight),
        [jax.ShapeDtypeStruct((own, rows, rows), F32), blocks(own, BF16)] + split_shapes(share)
        + [blocks(cap, BF16), blocks(cap, BF16)],
        [tiles(lcap), tiles(rounds * cap), room(own, BF16), tiles(own + 1, F32), room(cap + 1, F32), sems(3)],
        rounds * cap * tile_flops, (3,),
    )
    z_arrived = scattered(z_next, z_far, z_before)
    got_back_b = swapped(back_b, bits[1])
    got_back_a = swapped(back_a, bits[0])
    got_back_c = swapped(finished(z_own, z_arrived), bits[2])

    need_a, need_b, need_c, near = call(
        feat_kernel, (counts, lrows, lcols, sends, me), part_feats + (lv,),
        [blocks(cap, BF16), blocks(cap, BF16), blocks(share, BF16), blocks(own, F32)],
        [room(part, BF16), tiles(lcap), room(own + 1, F32), sems(6), sems(cap), sems(cap), sems(share)],
        lcap * tile_flops, (), range(3),
    )
    got_c = swapped(need_c, bits[2])
    got_b = swapped(need_b, bits[1])
    got_a = swapped(need_a, bits[0])

    right, left, keep_r, keep_l, own_part = call(
        merge_kernel, (counts, lrows, lcols, sends, me), (lv, gh, got_back_a, got_back_b, got_back_c),
        [blocks(own, BF16), blocks(own, BF16), blocks(half, F32), blocks(half, F32), blocks(own, F32)],
        [tiles(lcap), room(own, BF16), room(cap, BF16), room(cap, BF16), room(share, BF16), room(part + 1, F32), sems(5)],
        lcap * tile_flops,
    )
    a_left = shifted(right, 1)
    a_right = shifted(left, -1)

    def halves(start):
        return pl.BlockSpec((half,) + tail, lambda i: (start, 0, 0))

    out_r, out_l = pl.pallas_call(
        combine_kernel,
        out_shape=(blocks(half, BF16), blocks(half, BF16)),
        grid=(1,),
        in_specs=[halves(0)] * 4,
        out_specs=(halves(0), halves(0)),
        cost_estimate=pl.CostEstimate(flops=0, bytes_accessed=8 * half * rows * width, transcendentals=0),
    )(keep_r, keep_l, a_left, a_right)
    b_left = shifted(out_r, 1)
    b_right = shifted(out_l, -1)
    grad_features = pl.pallas_call(
        relay_finish_kernel,
        out_shape=blocks(own, BF16),
        grid=(1,),
        in_specs=[pl.BlockSpec((own,) + tail, lambda i: (0, 0, 0)), halves(1), halves(1), halves(0), halves(0)],
        out_specs=pl.BlockSpec((own,) + tail, lambda i: (0, 0, 0)),
        cost_estimate=pl.CostEstimate(flops=0, bytes_accessed=10 * own * rows * width, transcendentals=0),
    )(own_part, a_left, a_right, b_left, b_right)

    output = call(
        far_kernel, (counts, rrows, rslots, me),
        (got_a, got_b) + spread_direct(got_c) + (rv, near, deg, weight), [blocks(own, BF16)],
        [room(rounds * cap, BF16), tiles(rounds * cap), room(own + 1, F32), tiles(own, F32), sems(9)],
        rounds * cap * tile_flops, (9,),
    )[0]
    return (output.reshape(rows_dev, width), grad_features.reshape(rows_dev, width))


def solution(mesh):
    in_specs = (
        P(("node", "feat"), None),
        P(),
        P(("node", "feat"), None),
        P("node", "feat", None),
        P("node", "feat", None),
        P("node", "feat", None, None, None),
        P("node", "feat", None, None),
        P("node", "feat", None, None),
        P("node", "feat", None, None, None, None),
        P("node", None, None),
        P("node", "feat", None),
    )
    out_specs = (P(("node", "feat"), None), P(("node", "feat"), None))
    return jax.shard_map(body, mesh=mesh, in_specs=in_specs, out_specs=out_specs, check_vma=False)
```

```python
import jax
import jax.numpy as jnp
from jax import lax
from jax.experimental import pallas as pl
from jax.experimental.pallas import tpu as pltpu
from jax.sharding import PartitionSpec as P


UNROLL = 4
F32 = jnp.float32
BF16 = jnp.bfloat16
SMEM = pl.BlockSpec(memory_space=pltpu.SMEM)
VMEM = pl.BlockSpec(memory_space=pltpu.VMEM)
ANY = pl.BlockSpec(memory_space=pl.ANY)


def swapped(array, bit):
    return lax.ppermute(array, "node", [(i, i ^ 1 << bit) for i in range(lax.axis_size("node"))])


def shifted(array, step):
    size = lax.axis_size("feat")
    return lax.ppermute(array, "feat", [(i, (i + step) % size) for i in range(size)])


def spread_relayed(mine):
    half = mine.shape[0] // 2
    before = shifted(mine, 1)
    after = shifted(mine, -1)
    far_low = shifted(before[:half], 1)
    far_high = shifted(after[half:], -1)
    return (mine, after, far_low, far_high, before)


def spread_direct(mine):
    before = shifted(mine, 1)
    after = shifted(mine, -1)
    far = shifted(mine, 2)
    return (mine, after, far, before)


def scattered(to_next, to_far, to_before):
    return shifted(to_next, 1), shifted(to_far, 2), shifted(to_before, -1)


def start_all(pairs, sems):
    copies = [pltpu.make_async_copy(a, b, sems.at[i]) for i, (a, b) in enumerate(pairs)]
    for copy in copies:
        copy.start()
    return copies


def wait_all(copies):
    for copy in copies:
        copy.wait()


def pieces_into(pieces, dst, base):
    pairs = []
    for piece in pieces:
        pairs.append((piece, dst.at[pl.ds(base, piece.shape[0])]))
        base += piece.shape[0]
    return pairs


def for_live(count, step):
    def group(k, carry):
        for u in range(UNROLL):
            t = k * UNROLL + u
            step(t, t < count)
        return carry

    lax.fori_loop(0, pl.cdiv(count, UNROLL), group, 0)


def forward_tiles(count, base, vals, row_of, source_of, acc):
    trash = acc.shape[0] - 1

    def step(t, live):
        row = jnp.where(live, row_of(t), trash)
        acc[row] += jnp.dot(vals[base + t], source_of(t), preferred_element_type=F32)

    for_live(count, step)


def backward_tiles(count, base, vals, row_of, target_of, grads, acc):
    trash = acc.shape[0] - 1

    def step(t, live):
        target = jnp.where(live, target_of(t), trash)
        acc[target] += lax.dot_general(
            vals[base + t], grads[row_of(t)], (((0,), (0,)), ((), ())), preferred_element_type=F32
        )

    for_live(count, step)


def degree_kernel(counts, lrows, rrows, rslots, me, lv_hbm, rv_hbm, go_hbm, w_ref,
                  deg_ref, gh_ref, next_ref, far_ref, before_ref, own_ref,
                  lv, rv, go, dacc, acc, sems):
    copies = start_all([(lv_hbm, lv), (rv_hbm, rv), (go_hbm, go)], sems)
    own = deg_ref.shape[0]
    cap = rrows.shape[2]
    dacc[...] = jnp.zeros_like(dacc)
    acc[...] = jnp.zeros_like(acc)
    copies[0].wait()

    def add_rows(vals, base, row_of):
        def step(t, live):
            row = jnp.where(live, row_of(t), own)
            dacc[row] += vals[base + t].astype(F32)

        return step

    for_live(counts[0], add_rows(lv, 0, lambda t: lrows[t]))
    copies[1].wait()
    for r in range(rrows.shape[0]):
        for_live(counts[r + 1], add_rows(rv, r * cap, lambda t: rrows[r, 0, t]))
    copies[2].wait()
    for b in range(own):
        degree = 1.0 + jnp.broadcast_to(jnp.sum(dacc[b], axis=1, keepdims=True), dacc.shape[1:])
        deg_ref[b] = degree
        dense = lax.dot_general(go[b], w_ref[...], (((1,), (1,)), ((), ())), preferred_element_type=F32)
        width = degree.shape[1]
        for k in range(dense.shape[1] // width):
            gh_ref[b, :, k * width:(k + 1) * width] = (
                dense[:, k * width:(k + 1) * width] / degree
            ).astype(BF16)
    share = own_ref.shape[0]
    shift = me[0] * share
    backward_tiles(
        counts[3], 2 * cap, rv, lambda t: rrows[2, 0, t],
        lambda t: lax.rem(rslots[2, 0, t] - shift + cap, cap), gh_ref, acc,
    )
    split_out(acc, share, next_ref, far_ref, before_ref, own_ref)


def parcels_kernel(counts, rrows, rslots, rv_hbm, gh_hbm, out_b, out_a, rv, gh, acc, sems):
    cap = rrows.shape[2]
    copies = start_all([(rv_hbm.at[pl.ds(0, 2 * cap)], rv), (gh_hbm, gh)], sems)
    acc[...] = jnp.zeros_like(acc)
    wait_all(copies)
    for r, out in ((1, out_b), (0, out_a)):
        backward_tiles(
            counts[r + 1], r * cap, rv, lambda t: rrows[r, 0, t], lambda t: rslots[r, 0, t], gh, acc
        )
        out[...] = acc[:cap].astype(BF16)
        if r:
            acc[...] = jnp.zeros_like(acc)


def split_out(acc, n, next_ref, far_ref, before_ref, own_ref):
    next_ref[...] = acc[n:2 * n].astype(BF16)
    far_ref[...] = acc[2 * n:3 * n].astype(BF16)
    before_ref[...] = acc[3 * n:4 * n].astype(BF16)
    own_ref[...] = acc[:n]


def merge_kernel(counts, lrows, lcols, sends, me, lv_hbm, gh_hbm, a_hbm, b_hbm, c_hbm,
                 right_ref, left_ref, keep_r_ref, keep_l_ref, own_ref, lv, gh, got_a, got_b, got_c, acc, sems):
    copies = start_all([(lv_hbm, lv), (gh_hbm, gh), (a_hbm, got_a), (b_hbm, got_b), (c_hbm, got_c)], sems)
    own = gh.shape[0]
    total = acc.shape[0] - 1
    acc[own:] = jnp.zeros((total + 1 - own,) + acc.shape[1:], F32)
    wait_all(copies[:2])
    acc[:own] = gh[...].astype(F32)
    shift = me[0] * own
    backward_tiles(
        counts[0], 0, lv, lambda t: lrows[t],
        lambda t: lax.rem(lcols[t] - shift + total, total), gh, acc,
    )
    wait_all(copies[2:])
    for r, (got, base) in enumerate(((got_a, 0), (got_b, 0), (got_c, me[0] * got_c.shape[0]))):
        for s in range(got.shape[0]):
            acc[lax.rem(sends[r, 0, base + s] - shift + total, total)] += got[s].astype(F32)
    n, h = own, own // 2
    right_ref[:h] = acc[2 * n:2 * n + h].astype(BF16)
    right_ref[h:] = acc[n + h:2 * n].astype(BF16)
    left_ref[:h] = acc[2 * n + h:3 * n].astype(BF16)
    left_ref[h:] = acc[3 * n:3 * n + h].astype(BF16)
    keep_r_ref[...] = acc[n:n + h]
    keep_l_ref[...] = acc[3 * n + h:4 * n]
    own_ref[...] = acc[:n]


def combine_kernel(keep_r, keep_l, from_left, from_right, out_r, out_l):
    out_r[...] = (keep_r[...] + from_left[...].astype(F32)).astype(BF16)
    out_l[...] = (keep_l[...] + from_right[...].astype(F32)).astype(BF16)


def relay_finish_kernel(own, a_left, a_right, b_left, b_right, out):
    h = own.shape[0] // 2
    out[:h] = (own[:h] + a_right[...].astype(F32) + b_left[...].astype(F32)).astype(BF16)
    out[h:] = (own[h:] + a_left[...].astype(F32) + b_right[...].astype(F32)).astype(BF16)


def finish_kernel(own, a, b, c, out):
    out[...] = (own[...] + a[...].astype(F32) + b[...].astype(F32) + c[...].astype(F32)).astype(BF16)


def feat_kernel(counts, lrows, lcols, sends, me, p0, p1, p2, p3, p4, lv_hbm, out_a, out_b, near_ref,
                src, lv, acc, sems, sems_a, sems_b):
    copies = start_all(pieces_into((p0, p1, p2, p3, p4), src, 0) + [(lv_hbm, lv)], sems)
    total = src.shape[0]
    own = near_ref.shape[0]
    shift = me[0] * own
    wait_all(copies[:5])
    picks = ((out_b, 1, sems_b), (out_a, 0, sems_a))

    def begin(out, r, marks):
        def one(s, carry):
            at = lax.rem(sends[r, 0, s] - shift + total, total)
            pltpu.make_async_copy(src.at[at], out.at[s], marks.at[s]).start()
            return carry

        lax.fori_loop(0, out.shape[0], one, 0)

    def end(out, r, marks):
        def one(s, carry):
            pltpu.make_async_copy(src.at[0], out.at[s], marks.at[s]).wait()
            return carry

        lax.fori_loop(0, out.shape[0], one, 0)

    for pick in picks:
        begin(*pick)
    acc[:own] = src[:own].astype(F32)
    copies[5].wait()
    forward_tiles(
        counts[0], 0, lv, lambda t: lrows[t], lambda t: src[lax.rem(lcols[t] - shift + total, total)], acc
    )
    near_ref[...] = acc[:own]
    for pick in picks:
        end(*pick)


def far_kernel(counts, rrows, rslots, ids, me, a_hbm, b_hbm, p0, p1, p2, p3, rv_hbm, near_hbm, deg_hbm, w_ref,
               out_ref, src, vals, acc, deg, sems):
    total = out_ref.shape[0]
    cap = rrows.shape[2]
    pairs = [(near_hbm, acc.at[pl.ds(0, total)]), (rv_hbm, vals)]
    pairs += pieces_into((a_hbm, b_hbm, p0, p1, p2, p3), src, 0) + [(deg_hbm, deg)]
    wait_all(start_all(pairs, sems))
    for r in range(2):
        forward_tiles(
            counts[r + 1], r * cap, vals, lambda t: rrows[r, 0, t], lambda t: src[r * cap + rslots[r, 0, t]], acc
        )
    part = src.shape[0] - 2 * cap
    shift = me[0] * p0.shape[0]
    forward_tiles(
        counts[3], 2 * cap, vals, lambda t: rrows[2, 0, t],
        lambda t: src[2 * cap + lax.rem(ids[0, rslots[2, 0, t]] - shift + part, part)], acc,
    )
    width = deg.shape[2]
    for b in range(total):
        hidden = jnp.concatenate(
            [acc[b, :, k:k + width] / deg[b] for k in range(0, acc.shape[2], width)], axis=1
        ).astype(BF16)
        out_ref[b] = jnp.dot(hidden, w_ref[...], preferred_element_type=F32).astype(BF16)


def body(
    features,
    weight,
    grad_out,
    local_rows,
    local_cols,
    local_values,
    remote_rows,
    remote_slots,
    remote_values,
    send_blocks,
    tile_counts,
):
    rows_dev, width = features.shape
    lcap, rows = local_values.shape[2:4]
    own = rows_dev // rows
    rounds, cap = remote_rows.shape[2:]
    slices = lax.axis_size("feat")
    part = own * slices
    share = cap // slices
    half = own // 2
    log_nodes = lax.axis_size("node").bit_length() - 1
    bits = [r * log_nodes // rounds for r in range(rounds)]
    tail = (rows, width)

    me = lax.axis_index("feat").astype(jnp.int32).reshape(1)
    counts = tile_counts[0, 0]
    lrows, lcols = local_rows[0, 0], local_cols[0, 0]
    rrows, rslots, sends = (a.reshape(rounds, 1, cap) for a in (remote_rows, remote_slots, send_blocks))
    lv = local_values.reshape(lcap, rows, rows)
    rv = remote_values.reshape(rounds * cap, rows, rows)
    feats = features.reshape((own,) + tail)
    go = grad_out.reshape((own,) + tail)

    def blocks(n, kind):
        return jax.ShapeDtypeStruct((n,) + tail, kind)

    def room(n, kind):
        return pltpu.VMEM((n,) + tail, kind)

    def tiles(n, kind=BF16):
        return pltpu.VMEM((n, rows, rows), kind)

    def call(kernel, scalars, args, outs, scratch, flops, in_place=(), out_place=()):
        size = sum(a.size * a.dtype.itemsize for a in args)
        size += sum(o.size * o.dtype.itemsize for o in outs)
        return pl.pallas_call(
            kernel,
            out_shape=tuple(outs),
            in_specs=[SMEM] * len(scalars) + [VMEM if i in in_place else ANY for i in range(len(args))],
            out_specs=tuple(ANY if i in out_place else VMEM for i in range(len(outs))),
            scratch_shapes=scratch,
            cost_estimate=pl.CostEstimate(flops=flops, bytes_accessed=size, transcendentals=0),
        )(*scalars, *args)

    def sems(n):
        return pltpu.SemaphoreType.DMA((n,))

    tile_flops = 2 * rows * rows * width

    def split_shapes(n):
        return [blocks(n, BF16), blocks(n, BF16), blocks(n, BF16), blocks(n, F32)]

    def finished(own_part, arrived):
        n = own_part.shape[0]
        return call(finish_kernel, (), (own_part,) + arrived, [blocks(n, BF16)], [], 0, range(4))[0]

    part_feats = spread_relayed(feats)
    partner_feats = spread_direct(swapped(feats, bits[2]))
    ids = swapped(sends[2], bits[2])

    deg, gh, z_next, z_far, z_before, z_own = call(
        degree_kernel, (counts, lrows, rrows, rslots, me), (lv, rv, go, weight),
        [jax.ShapeDtypeStruct((own, rows, rows), F32), blocks(own, BF16)] + split_shapes(share),
        [tiles(lcap), tiles(rounds * cap), room(own, BF16), tiles(own + 1, F32), room(cap + 1, F32), sems(3)],
        cap * tile_flops, (3,),
    )
    back_b, back_a = call(
        parcels_kernel, (counts, rrows, rslots), (rv, gh), [blocks(cap, BF16), blocks(cap, BF16)],
        [tiles(2 * cap), room(own, BF16), room(cap + 1, F32), sems(2)], 2 * cap * tile_flops,
    )
    z_arrived = scattered(z_next, z_far, z_before)
    got_back_b = swapped(back_b, bits[1])
    got_back_a = swapped(back_a, bits[0])
    got_back_c = swapped(finished(z_own, z_arrived), bits[2])

    need_a, need_b, near = call(
        feat_kernel, (counts, lrows, lcols, sends, me), part_feats + (lv,),
        [blocks(cap, BF16), blocks(cap, BF16), blocks(own, F32)],
        [room(part, BF16), tiles(lcap), room(own + 1, F32), sems(6), sems(cap), sems(cap)],
        lcap * tile_flops, (), range(2),
    )
    got_b = swapped(need_b, bits[1])
    got_a = swapped(need_a, bits[0])

    right, left, keep_r, keep_l, own_part = call(
        merge_kernel, (counts, lrows, lcols, sends, me), (lv, gh, got_back_a, got_back_b, got_back_c),
        [blocks(own, BF16), blocks(own, BF16), blocks(half, F32), blocks(half, F32), blocks(own, F32)],
        [tiles(lcap), room(own, BF16), room(cap, BF16), room(cap, BF16), room(share, BF16), room(part + 1, F32), sems(5)],
        lcap * tile_flops,
    )
    a_left = shifted(right, 1)
    a_right = shifted(left, -1)

    def halves(start):
        return pl.BlockSpec((half,) + tail, lambda i: (start, 0, 0))

    out_r, out_l = pl.pallas_call(
        combine_kernel,
        out_shape=(blocks(half, BF16), blocks(half, BF16)),
        grid=(1,),
        in_specs=[halves(0)] * 4,
        out_specs=(halves(0), halves(0)),
        cost_estimate=pl.CostEstimate(flops=0, bytes_accessed=8 * half * rows * width, transcendentals=0),
    )(keep_r, keep_l, a_left, a_right)
    b_left = shifted(out_r, 1)
    b_right = shifted(out_l, -1)
    grad_features = pl.pallas_call(
        relay_finish_kernel,
        out_shape=blocks(own, BF16),
        grid=(1,),
        in_specs=[pl.BlockSpec((own,) + tail, lambda i: (0, 0, 0)), halves(1), halves(1), halves(0), halves(0)],
        out_specs=pl.BlockSpec((own,) + tail, lambda i: (0, 0, 0)),
        cost_estimate=pl.CostEstimate(flops=0, bytes_accessed=10 * own * rows * width, transcendentals=0),
    )(own_part, a_left, a_right, b_left, b_right)

    output = call(
        far_kernel, (counts, rrows, rslots, ids, me),
        (got_a, got_b) + partner_feats + (rv, near, deg, weight), [blocks(own, BF16)],
        [room(2 * cap + part, BF16), tiles(rounds * cap), room(own + 1, F32), tiles(own, F32), sems(9)],
        rounds * cap * tile_flops, (9,),
    )[0]
    return (output.reshape(rows_dev, width), grad_features.reshape(rows_dev, width))


def solution(mesh):
    in_specs = (
        P(("node", "feat"), None),
        P(),
        P(("node", "feat"), None),
        P("node", "feat", None),
        P("node", "feat", None),
        P("node", "feat", None, None, None),
        P("node", "feat", None, None),
        P("node", "feat", None, None),
        P("node", "feat", None, None, None, None),
        P("node", None, None),
        P("node", "feat", None),
    )
    out_specs = (P(("node", "feat"), None), P(("node", "feat"), None))
    return jax.shard_map(body, mesh=mesh, in_specs=in_specs, out_specs=out_specs, check_vma=False)
```

```python
import jax
import jax.numpy as jnp
from jax import lax
from jax.experimental import pallas as pl
from jax.experimental.pallas import tpu as pltpu
from jax.sharding import PartitionSpec as P


UNROLL = 4
F32 = jnp.float32
BF16 = jnp.bfloat16
SMEM = pl.BlockSpec(memory_space=pltpu.SMEM)
VMEM = pl.BlockSpec(memory_space=pltpu.VMEM)
ANY = pl.BlockSpec(memory_space=pl.ANY)


def swapped(array, bit):
    return lax.ppermute(array, "node", [(i, i ^ 1 << bit) for i in range(lax.axis_size("node"))])


def shifted(array, step):
    size = lax.axis_size("feat")
    return lax.ppermute(array, "feat", [(i, (i + step) % size) for i in range(size)])


def spread_relayed(mine):
    half = mine.shape[0] // 2
    before = shifted(mine, 1)
    after = shifted(mine, -1)
    far_low = shifted(before[:half], 1)
    far_high = shifted(after[half:], -1)
    return (mine, after, far_low, far_high, before)


def scattered(to_next, to_far, to_before):
    return shifted(to_next, 1), shifted(to_far, 2), shifted(to_before, -1)


def start_all(pairs, sems):
    copies = [pltpu.make_async_copy(a, b, sems.at[i]) for i, (a, b) in enumerate(pairs)]
    for copy in copies:
        copy.start()
    return copies


def wait_all(copies):
    for copy in copies:
        copy.wait()


def pieces_into(pieces, dst, base):
    pairs = []
    for piece in pieces:
        pairs.append((piece, dst.at[pl.ds(base, piece.shape[0])]))
        base += piece.shape[0]
    return pairs


def for_live(count, step):
    def group(k, carry):
        for u in range(UNROLL):
            t = k * UNROLL + u
            step(t, t < count)
        return carry

    lax.fori_loop(0, pl.cdiv(count, UNROLL), group, 0)


def forward_tiles(count, base, vals, row_of, source_of, acc):
    trash = acc.shape[0] - 1

    def step(t, live):
        row = jnp.where(live, row_of(t), trash)
        acc[row] += jnp.dot(vals[base + t], source_of(t), preferred_element_type=F32)

    for_live(count, step)


def backward_tiles(count, base, vals, row_of, target_of, grads, acc):
    trash = acc.shape[0] - 1

    def step(t, live):
        target = jnp.where(live, target_of(t), trash)
        acc[target] += lax.dot_general(
            vals[base + t], grads[row_of(t)], (((0,), (0,)), ((), ())), preferred_element_type=F32
        )

    for_live(count, step)


def degree_kernel(counts, lrows, rrows, rslots, me, lv_hbm, rv_hbm, go_hbm, w_ref,
                  deg_ref, gh_ref, next_ref, far_ref, before_ref, own_ref,
                  lv, rv, go, dacc, acc, sems):
    copies = start_all([(lv_hbm, lv), (rv_hbm, rv), (go_hbm, go)], sems)
    own = deg_ref.shape[0]
    cap = rrows.shape[2]
    dacc[...] = jnp.zeros_like(dacc)
    acc[...] = jnp.zeros_like(acc)
    copies[0].wait()

    def add_rows(vals, base, row_of):
        def step(t, live):
            row = jnp.where(live, row_of(t), own)
            dacc[row] += vals[base + t].astype(F32)

        return step

    for_live(counts[0], add_rows(lv, 0, lambda t: lrows[t]))
    copies[1].wait()
    for r in range(rrows.shape[0]):
        for_live(counts[r + 1], add_rows(rv, r * cap, lambda t: rrows[r, 0, t]))
    copies[2].wait()
    for b in range(own):
        degree = 1.0 + jnp.broadcast_to(jnp.sum(dacc[b], axis=1, keepdims=True), dacc.shape[1:])
        deg_ref[b] = degree
        dense = lax.dot_general(go[b], w_ref[...], (((1,), (1,)), ((), ())), preferred_element_type=F32)
        width = degree.shape[1]
        for k in range(dense.shape[1] // width):
            gh_ref[b, :, k * width:(k + 1) * width] = (
                dense[:, k * width:(k + 1) * width] / degree
            ).astype(BF16)
    share = own_ref.shape[0]
    shift = me[0] * share
    backward_tiles(
        counts[3], 2 * cap, rv, lambda t: rrows[2, 0, t],
        lambda t: lax.rem(rslots[2, 0, t] - shift + cap, cap), gh_ref, acc,
    )
    split_out(acc, share, next_ref, far_ref, before_ref, own_ref)


def parcels_kernel(counts, rrows, rslots, rv_hbm, gh_hbm, out_b, out_a, rv, gh, acc, sems):
    cap = rrows.shape[2]
    copies = start_all([(rv_hbm.at[pl.ds(0, 2 * cap)], rv), (gh_hbm, gh)], sems)
    acc[...] = jnp.zeros_like(acc)
    wait_all(copies)
    for r, out in ((1, out_b), (0, out_a)):
        backward_tiles(
            counts[r + 1], r * cap, rv, lambda t: rrows[r, 0, t], lambda t: rslots[r, 0, t], gh, acc
        )
        out[...] = acc[:cap].astype(BF16)
        if r:
            acc[...] = jnp.zeros_like(acc)


def split_out(acc, n, next_ref, far_ref, before_ref, own_ref):
    next_ref[...] = acc[n:2 * n].astype(BF16)
    far_ref[...] = acc[2 * n:3 * n].astype(BF16)
    before_ref[...] = acc[3 * n:4 * n].astype(BF16)
    own_ref[...] = acc[:n]


def merge_kernel(counts, lrows, lcols, sends, me, lv_hbm, gh_hbm, a_hbm, b_hbm, c_hbm,
                 right_ref, left_ref, keep_r_ref, keep_l_ref, own_ref, lv, gh, got_a, got_b, got_c, acc, sems):
    copies = start_all([(lv_hbm, lv), (gh_hbm, gh), (a_hbm, got_a), (b_hbm, got_b), (c_hbm, got_c)], sems)
    own = gh.shape[0]
    total = acc.shape[0] - 1
    acc[own:] = jnp.zeros((total + 1 - own,) + acc.shape[1:], F32)
    wait_all(copies[:2])
    acc[:own] = gh[...].astype(F32)
    shift = me[0] * own
    backward_tiles(
        counts[0], 0, lv, lambda t: lrows[t],
        lambda t: lax.rem(lcols[t] - shift + total, total), gh, acc,
    )
    wait_all(copies[2:])
    for r, (got, base) in enumerate(((got_a, 0), (got_b, 0), (got_c, me[0] * got_c.shape[0]))):
        for s in range(got.shape[0]):
            acc[lax.rem(sends[r, 0, base + s] - shift + total, total)] += got[s].astype(F32)
    n, h = own, own // 2
    right_ref[:h] = acc[2 * n:2 * n + h].astype(BF16)
    right_ref[h:] = acc[n + h:2 * n].astype(BF16)
    left_ref[:h] = acc[2 * n + h:3 * n].astype(BF16)
    left_ref[h:] = acc[3 * n:3 * n + h].astype(BF16)
    keep_r_ref[...] = acc[n:n + h]
    keep_l_ref[...] = acc[3 * n + h:4 * n]
    own_ref[...] = acc[:n]


def combine_kernel(keep_r, keep_l, from_left, from_right, out_r, out_l):
    out_r[...] = (keep_r[...] + from_left[...].astype(F32)).astype(BF16)
    out_l[...] = (keep_l[...] + from_right[...].astype(F32)).astype(BF16)


def relay_finish_kernel(own, a_left, a_right, b_left, b_right, out):
    h = own.shape[0] // 2
    out[:h] = (own[:h] + a_right[...].astype(F32) + b_left[...].astype(F32)).astype(BF16)
    out[h:] = (own[h:] + a_left[...].astype(F32) + b_right[...].astype(F32)).astype(BF16)


def finish_kernel(own, a, b, c, out):
    out[...] = (own[...] + a[...].astype(F32) + b[...].astype(F32) + c[...].astype(F32)).astype(BF16)


def feat_kernel(counts, lrows, lcols, sends, me, p0, p1, p2, p3, p4, lv_hbm, out_a, out_b, near_ref,
                src, lv, acc, sems, sems_a, sems_b):
    copies = start_all(pieces_into((p0, p1, p2, p3, p4), src, 0) + [(lv_hbm, lv)], sems)
    total = src.shape[0]
    own = near_ref.shape[0]
    shift = me[0] * own
    wait_all(copies[:5])
    picks = ((out_b, 1, sems_b), (out_a, 0, sems_a))

    def begin(out, r, marks):
        def one(s, carry):
            at = lax.rem(sends[r, 0, s] - shift + total, total)
            pltpu.make_async_copy(src.at[at], out.at[s], marks.at[s]).start()
            return carry

        lax.fori_loop(0, out.shape[0], one, 0)

    def end(out, r, marks):
        def one(s, carry):
            pltpu.make_async_copy(src.at[0], out.at[s], marks.at[s]).wait()
            return carry

        lax.fori_loop(0, out.shape[0], one, 0)

    for pick in picks:
        begin(*pick)
    acc[:own] = src[:own].astype(F32)
    copies[5].wait()
    forward_tiles(
        counts[0], 0, lv, lambda t: lrows[t], lambda t: src[lax.rem(lcols[t] - shift + total, total)], acc
    )
    near_ref[...] = acc[:own]
    for pick in picks:
        end(*pick)


def far_kernel(counts, rrows, rslots, ids, me, a_hbm, b_hbm, p0, p1, p2, p3, p4, rv_hbm, near_hbm, deg_hbm, w_ref,
               out_ref, src, vals, acc, deg, sems):
    total = out_ref.shape[0]
    cap = rrows.shape[2]
    pairs = [(near_hbm, acc.at[pl.ds(0, total)]), (rv_hbm, vals)]
    pairs += pieces_into((a_hbm, b_hbm, p0, p1, p2, p3, p4), src, 0) + [(deg_hbm, deg)]
    wait_all(start_all(pairs, sems))
    for r in range(2):
        forward_tiles(
            counts[r + 1], r * cap, vals, lambda t: rrows[r, 0, t], lambda t: src[r * cap + rslots[r, 0, t]], acc
        )
    part = src.shape[0] - 2 * cap
    shift = me[0] * p0.shape[0]
    forward_tiles(
        counts[3], 2 * cap, vals, lambda t: rrows[2, 0, t],
        lambda t: src[2 * cap + lax.rem(ids[0, rslots[2, 0, t]] - shift + part, part)], acc,
    )
    width = deg.shape[2]
    for b in range(total):
        hidden = jnp.concatenate(
            [acc[b, :, k:k + width] / deg[b] for k in range(0, acc.shape[2], width)], axis=1
        ).astype(BF16)
        out_ref[b] = jnp.dot(hidden, w_ref[...], preferred_element_type=F32).astype(BF16)


def body(
    features,
    weight,
    grad_out,
    local_rows,
    local_cols,
    local_values,
    remote_rows,
    remote_slots,
    remote_values,
    send_blocks,
    tile_counts,
):
    rows_dev, width = features.shape
    lcap, rows = local_values.shape[2:4]
    own = rows_dev // rows
    rounds, cap = remote_rows.shape[2:]
    slices = lax.axis_size("feat")
    part = own * slices
    share = cap // slices
    half = own // 2
    log_nodes = lax.axis_size("node").bit_length() - 1
    bits = [r * log_nodes // rounds for r in range(rounds)]
    tail = (rows, width)

    me = lax.axis_index("feat").astype(jnp.int32).reshape(1)
    counts = tile_counts[0, 0]
    lrows, lcols = local_rows[0, 0], local_cols[0, 0]
    rrows, rslots, sends = (a.reshape(rounds, 1, cap) for a in (remote_rows, remote_slots, send_blocks))
    lv = local_values.reshape(lcap, rows, rows)
    rv = remote_values.reshape(rounds * cap, rows, rows)
    feats = features.reshape((own,) + tail)
    go = grad_out.reshape((own,) + tail)

    def blocks(n, kind):
        return jax.ShapeDtypeStruct((n,) + tail, kind)

    def room(n, kind):
        return pltpu.VMEM((n,) + tail, kind)

    def tiles(n, kind=BF16):
        return pltpu.VMEM((n, rows, rows), kind)

    def call(kernel, scalars, args, outs, scratch, flops, in_place=(), out_place=()):
        size = sum(a.size * a.dtype.itemsize for a in args)
        size += sum(o.size * o.dtype.itemsize for o in outs)
        return pl.pallas_call(
            kernel,
            out_shape=tuple(outs),
            in_specs=[SMEM] * len(scalars) + [VMEM if i in in_place else ANY for i in range(len(args))],
            out_specs=tuple(ANY if i in out_place else VMEM for i in range(len(outs))),
            scratch_shapes=scratch,
            cost_estimate=pl.CostEstimate(flops=flops, bytes_accessed=size, transcendentals=0),
        )(*scalars, *args)

    def sems(n):
        return pltpu.SemaphoreType.DMA((n,))

    tile_flops = 2 * rows * rows * width

    def split_shapes(n):
        return [blocks(n, BF16), blocks(n, BF16), blocks(n, BF16), blocks(n, F32)]

    def finished(own_part, arrived):
        n = own_part.shape[0]
        return call(finish_kernel, (), (own_part,) + arrived, [blocks(n, BF16)], [], 0, range(4))[0]

    part_feats = spread_relayed(feats)
    partner_feats = spread_relayed(swapped(feats, bits[2]))
    ids = swapped(sends[2], bits[2])

    deg, gh, z_next, z_far, z_before, z_own = call(
        degree_kernel, (counts, lrows, rrows, rslots, me), (lv, rv, go, weight),
        [jax.ShapeDtypeStruct((own, rows, rows), F32), blocks(own, BF16)] + split_shapes(share),
        [tiles(lcap), tiles(rounds * cap), room(own, BF16), tiles(own + 1, F32), room(cap + 1, F32), sems(3)],
        cap * tile_flops, (3,),
    )
    back_b, back_a = call(
        parcels_kernel, (counts, rrows, rslots), (rv, gh), [blocks(cap, BF16), blocks(cap, BF16)],
        [tiles(2 * cap), room(own, BF16), room(cap + 1, F32), sems(2)], 2 * cap * tile_flops,
    )
    z_arrived = scattered(z_next, z_far, z_before)
    got_back_b = swapped(back_b, bits[1])
    got_back_a = swapped(back_a, bits[0])
    got_back_c = swapped(finished(z_own, z_arrived), bits[2])

    need_a, need_b, near = call(
        feat_kernel, (counts, lrows, lcols, sends, me), part_feats + (lv,),
        [blocks(cap, BF16), blocks(cap, BF16), blocks(own, F32)],
        [room(part, BF16), tiles(lcap), room(own + 1, F32), sems(6), sems(cap), sems(cap)],
        lcap * tile_flops, (), range(2),
    )
    got_b = swapped(need_b, bits[1])
    got_a = swapped(need_a, bits[0])

    right, left, keep_r, keep_l, own_part = call(
        merge_kernel, (counts, lrows, lcols, sends, me), (lv, gh, got_back_a, got_back_b, got_back_c),
        [blocks(own, BF16), blocks(own, BF16), blocks(half, F32), blocks(half, F32), blocks(own, F32)],
        [tiles(lcap), room(own, BF16), room(cap, BF16), room(cap, BF16), room(share, BF16), room(part + 1, F32), sems(5)],
        lcap * tile_flops,
    )
    a_left = shifted(right, 1)
    a_right = shifted(left, -1)

    def halves(start):
        return pl.BlockSpec((half,) + tail, lambda i: (start, 0, 0))

    out_r, out_l = pl.pallas_call(
        combine_kernel,
        out_shape=(blocks(half, BF16), blocks(half, BF16)),
        grid=(1,),
        in_specs=[halves(0)] * 4,
        out_specs=(halves(0), halves(0)),
        cost_estimate=pl.CostEstimate(flops=0, bytes_accessed=8 * half * rows * width, transcendentals=0),
    )(keep_r, keep_l, a_left, a_right)
    b_left = shifted(out_r, 1)
    b_right = shifted(out_l, -1)
    grad_features = pl.pallas_call(
        relay_finish_kernel,
        out_shape=blocks(own, BF16),
        grid=(1,),
        in_specs=[pl.BlockSpec((own,) + tail, lambda i: (0, 0, 0)), halves(1), halves(1), halves(0), halves(0)],
        out_specs=pl.BlockSpec((own,) + tail, lambda i: (0, 0, 0)),
        cost_estimate=pl.CostEstimate(flops=0, bytes_accessed=10 * own * rows * width, transcendentals=0),
    )(own_part, a_left, a_right, b_left, b_right)

    output = call(
        far_kernel, (counts, rrows, rslots, ids, me),
        (got_a, got_b) + partner_feats + (rv, near, deg, weight), [blocks(own, BF16)],
        [room(2 * cap + part, BF16), tiles(rounds * cap), room(own + 1, F32), tiles(own, F32), sems(10)],
        rounds * cap * tile_flops, (10,),
    )[0]
    return (output.reshape(rows_dev, width), grad_features.reshape(rows_dev, width))


def solution(mesh):
    in_specs = (
        P(("node", "feat"), None),
        P(),
        P(("node", "feat"), None),
        P("node", "feat", None),
        P("node", "feat", None),
        P("node", "feat", None, None, None),
        P("node", "feat", None, None),
        P("node", "feat", None, None),
        P("node", "feat", None, None, None, None),
        P("node", None, None),
        P("node", "feat", None),
    )
    out_specs = (P(("node", "feat"), None), P(("node", "feat"), None))
    return jax.shard_map(body, mesh=mesh, in_specs=in_specs, out_specs=out_specs, check_vma=False)
```

```python
import jax
import jax.numpy as jnp
from jax import lax
from jax.experimental import pallas as pl
from jax.experimental.pallas import tpu as pltpu
from jax.sharding import PartitionSpec as P


UNROLL = 4
F32 = jnp.float32
BF16 = jnp.bfloat16
SMEM = pl.BlockSpec(memory_space=pltpu.SMEM)
VMEM = pl.BlockSpec(memory_space=pltpu.VMEM)
ANY = pl.BlockSpec(memory_space=pl.ANY)


def swapped(array, bit):
    return lax.ppermute(array, "node", [(i, i ^ 1 << bit) for i in range(lax.axis_size("node"))])


def shifted(array, step):
    size = lax.axis_size("feat")
    return lax.ppermute(array, "feat", [(i, (i + step) % size) for i in range(size)])


def spread_relayed(mine):
    half = mine.shape[0] // 2
    before = shifted(mine, 1)
    after = shifted(mine, -1)
    far_low = shifted(before[:half], 1)
    far_high = shifted(after[half:], -1)
    return (mine, after, far_low, far_high, before)


def scattered(to_next, to_far, to_before):
    return shifted(to_next, 1), shifted(to_far, 2), shifted(to_before, -1)


def start_all(pairs, sems):
    copies = [pltpu.make_async_copy(a, b, sems.at[i]) for i, (a, b) in enumerate(pairs)]
    for copy in copies:
        copy.start()
    return copies


def wait_all(copies):
    for copy in copies:
        copy.wait()


def pieces_into(pieces, dst, base):
    pairs = []
    for piece in pieces:
        pairs.append((piece, dst.at[pl.ds(base, piece.shape[0])]))
        base += piece.shape[0]
    return pairs


def for_live(count, step):
    def group(k, carry):
        for u in range(UNROLL):
            t = k * UNROLL + u
            step(t, t < count)
        return carry

    lax.fori_loop(0, pl.cdiv(count, UNROLL), group, 0)


def forward_tiles(count, base, vals, row_of, source_of, acc):
    trash = acc.shape[0] - 1

    def step(t, live):
        row = jnp.where(live, row_of(t), trash)
        acc[row] += jnp.dot(vals[base + t], source_of(t), preferred_element_type=F32)

    for_live(count, step)


def backward_tiles(count, base, vals, row_of, target_of, grads, acc):
    trash = acc.shape[0] - 1

    def step(t, live):
        target = jnp.where(live, target_of(t), trash)
        acc[target] += lax.dot_general(
            vals[base + t], grads[row_of(t)], (((0,), (0,)), ((), ())), preferred_element_type=F32
        )

    for_live(count, step)


def degree_kernel(counts, lrows, rrows, rslots, me, lv_hbm, rv_hbm, go_hbm, w_ref,
                  deg_ref, gh_ref, next_ref, far_ref, before_ref, own_ref,
                  lv, rv, go, dacc, acc, sems):
    copies = start_all([(lv_hbm, lv), (rv_hbm, rv), (go_hbm, go)], sems)
    own = deg_ref.shape[0]
    cap = rrows.shape[2]
    dacc[...] = jnp.zeros_like(dacc)
    acc[...] = jnp.zeros_like(acc)
    copies[0].wait()

    def add_rows(vals, base, row_of):
        def step(t, live):
            row = jnp.where(live, row_of(t), own)
            dacc[row] += vals[base + t].astype(F32)

        return step

    for_live(counts[0], add_rows(lv, 0, lambda t: lrows[t]))
    copies[1].wait()
    for r in range(rrows.shape[0]):
        for_live(counts[r + 1], add_rows(rv, r * cap, lambda t: rrows[r, 0, t]))
    copies[2].wait()
    for b in range(own):
        degree = 1.0 + jnp.broadcast_to(jnp.sum(dacc[b], axis=1, keepdims=True), dacc.shape[1:])
        deg_ref[b] = degree
        dense = lax.dot_general(go[b], w_ref[...], (((1,), (1,)), ((), ())), preferred_element_type=F32)
        width = degree.shape[1]
        for k in range(dense.shape[1] // width):
            gh_ref[b, :, k * width:(k + 1) * width] = (
                dense[:, k * width:(k + 1) * width] / degree
            ).astype(BF16)
    share = own_ref.shape[0]
    shift = me[0] * share
    backward_tiles(
        counts[3], 2 * cap, rv, lambda t: rrows[2, 0, t],
        lambda t: lax.rem(rslots[2, 0, t] - shift + cap, cap), gh_ref, acc,
    )
    split_out(acc, share, next_ref, far_ref, before_ref, own_ref)


def parcels_kernel(counts, rrows, rslots, rv_hbm, gh_hbm, out_b, out_a, rv, gh, acc, sems):
    cap = rrows.shape[2]
    copies = start_all([(rv_hbm.at[pl.ds(0, 2 * cap)], rv), (gh_hbm, gh)], sems)
    acc[...] = jnp.zeros_like(acc)
    wait_all(copies)
    for r, out in ((1, out_b), (0, out_a)):
        backward_tiles(
            counts[r + 1], r * cap, rv, lambda t: rrows[r, 0, t], lambda t: rslots[r, 0, t], gh, acc
        )
        out[...] = acc[:cap].astype(BF16)
        if r:
            acc[...] = jnp.zeros_like(acc)


def split_out(acc, n, next_ref, far_ref, before_ref, own_ref):
    next_ref[...] = acc[n:2 * n].astype(BF16)
    far_ref[...] = acc[2 * n:3 * n].astype(BF16)
    before_ref[...] = acc[3 * n:4 * n].astype(BF16)
    own_ref[...] = acc[:n]


def merge_kernel(counts, lrows, lcols, sends, me, lv_hbm, gh_hbm, a_hbm, b_hbm, c_hbm,
                 right_ref, left_ref, keep_r_ref, keep_l_ref, own_ref, lv, gh, got_a, got_b, got_c, acc, sems):
    copies = start_all([(lv_hbm, lv), (gh_hbm, gh), (a_hbm, got_a), (b_hbm, got_b), (c_hbm, got_c)], sems)
    own = gh.shape[0]
    total = acc.shape[0] - 1
    acc[own:] = jnp.zeros((total + 1 - own,) + acc.shape[1:], F32)
    wait_all(copies[:2])
    acc[:own] = gh[...].astype(F32)
    shift = me[0] * own
    backward_tiles(
        counts[0], 0, lv, lambda t: lrows[t],
        lambda t: lax.rem(lcols[t] - shift + total, total), gh, acc,
    )
    wait_all(copies[2:])
    for r, (got, base) in enumerate(((got_a, 0), (got_b, 0), (got_c, me[0] * got_c.shape[0]))):
        for s in range(got.shape[0]):
            acc[lax.rem(sends[r, 0, base + s] - shift + total, total)] += got[s].astype(F32)
    n, h = own, own // 2
    right_ref[:h] = acc[2 * n:2 * n + h].astype(BF16)
    right_ref[h:] = acc[n + h:2 * n].astype(BF16)
    left_ref[:h] = acc[2 * n + h:3 * n].astype(BF16)
    left_ref[h:] = acc[3 * n:3 * n + h].astype(BF16)
    keep_r_ref[...] = acc[n:n + h]
    keep_l_ref[...] = acc[3 * n + h:4 * n]
    own_ref[...] = acc[:n]


def combine_kernel(keep_r, keep_l, from_left, from_right, out_r, out_l):
    out_r[...] = (keep_r[...] + from_left[...].astype(F32)).astype(BF16)
    out_l[...] = (keep_l[...] + from_right[...].astype(F32)).astype(BF16)


def relay_finish_kernel(own, a_left, a_right, b_left, b_right, out):
    h = own.shape[0] // 2
    out[:h] = (own[:h] + a_right[...].astype(F32) + b_left[...].astype(F32)).astype(BF16)
    out[h:] = (own[h:] + a_left[...].astype(F32) + b_right[...].astype(F32)).astype(BF16)


def finish_kernel(own, a, b, c, out):
    out[...] = (own[...] + a[...].astype(F32) + b[...].astype(F32) + c[...].astype(F32)).astype(BF16)


def feat_kernel(counts, lrows, lcols, sends, me, p0, p1, p2, p3, p4, lv_hbm, out_a, out_b, near_ref,
                src, lv, acc, sems, sems_a, sems_b):
    copies = start_all(pieces_into((p0, p1, p2, p3, p4), src, 0) + [(lv_hbm, lv)], sems)
    total = src.shape[0]
    own = near_ref.shape[0]
    shift = me[0] * own
    wait_all(copies[:5])
    picks = ((out_b, 1, sems_b), (out_a, 0, sems_a))

    def begin(out, r, marks):
        def one(s, carry):
            at = lax.rem(sends[r, 0, s] - shift + total, total)
            pltpu.make_async_copy(src.at[at], out.at[s], marks.at[s]).start()
            return carry

        lax.fori_loop(0, out.shape[0], one, 0)

    def end(out, r, marks):
        def one(s, carry):
            pltpu.make_async_copy(src.at[0], out.at[s], marks.at[s]).wait()
            return carry

        lax.fori_loop(0, out.shape[0], one, 0)

    for pick in picks:
        begin(*pick)
    acc[:own] = src[:own].astype(F32)
    copies[5].wait()
    forward_tiles(
        counts[0], 0, lv, lambda t: lrows[t], lambda t: src[lax.rem(lcols[t] - shift + total, total)], acc
    )
    near_ref[...] = acc[:own]
    for pick in picks:
        end(*pick)


def mid_kernel(counts, rrows, rslots, ids, me, a_hbm, p0, p1, p2, p3, p4, rv_hbm, near_hbm,
               out_ref, src, vals, acc, sems):
    total = out_ref.shape[0]
    cap = rrows.shape[2]
    part = src.shape[0] - cap
    pairs = [(near_hbm, acc.at[pl.ds(0, total)])]
    pairs += [(rv_hbm.at[pl.ds(0, cap)], vals.at[pl.ds(0, cap)])]
    pairs += [(rv_hbm.at[pl.ds(2 * cap, cap)], vals.at[pl.ds(cap, cap)])]
    pairs += pieces_into((a_hbm, p0, p1, p2, p3, p4), src, 0)
    wait_all(start_all(pairs, sems))
    forward_tiles(counts[1], 0, vals, lambda t: rrows[0, 0, t], lambda t: src[rslots[0, 0, t]], acc)
    shift = me[0] * p0.shape[0]
    forward_tiles(
        counts[3], cap, vals, lambda t: rrows[2, 0, t],
        lambda t: src[cap + lax.rem(ids[2, 0, rslots[2, 0, t]] - shift + part, part)], acc,
    )
    out_ref[...] = acc[:total]


def far_kernel(counts, rrows, rslots, b_hbm, rv_hbm, near_hbm, deg_hbm, w_ref, out_ref, src, vals, acc, deg, sems):
    total = out_ref.shape[0]
    cap = rrows.shape[2]
    pairs = [
        (near_hbm, acc.at[pl.ds(0, total)]), (rv_hbm.at[pl.ds(cap, cap)], vals), (b_hbm, src), (deg_hbm, deg)
    ]
    wait_all(start_all(pairs, sems))
    forward_tiles(counts[2], 0, vals, lambda t: rrows[1, 0, t], lambda t: src[rslots[1, 0, t]], acc)
    width = deg.shape[2]
    for b in range(total):
        hidden = jnp.concatenate(
            [acc[b, :, k:k + width] / deg[b] for k in range(0, acc.shape[2], width)], axis=1
        ).astype(BF16)
        out_ref[b] = jnp.dot(hidden, w_ref[...], preferred_element_type=F32).astype(BF16)


def body(
    features,
    weight,
    grad_out,
    local_rows,
    local_cols,
    local_values,
    remote_rows,
    remote_slots,
    remote_values,
    send_blocks,
    tile_counts,
):
    rows_dev, width = features.shape
    lcap, rows = local_values.shape[2:4]
    own = rows_dev // rows
    rounds, cap = remote_rows.shape[2:]
    slices = lax.axis_size("feat")
    part = own * slices
    share = cap // slices
    half = own // 2
    log_nodes = lax.axis_size("node").bit_length() - 1
    bits = [r * log_nodes // rounds for r in range(rounds)]
    tail = (rows, width)

    me = lax.axis_index("feat").astype(jnp.int32).reshape(1)
    counts = tile_counts[0, 0]
    lrows, lcols = local_rows[0, 0], local_cols[0, 0]
    rrows, rslots, sends = (a.reshape(rounds, 1, cap) for a in (remote_rows, remote_slots, send_blocks))
    lv = local_values.reshape(lcap, rows, rows)
    rv = remote_values.reshape(rounds * cap, rows, rows)
    feats = features.reshape((own,) + tail)
    go = grad_out.reshape((own,) + tail)

    def blocks(n, kind):
        return jax.ShapeDtypeStruct((n,) + tail, kind)

    def room(n, kind):
        return pltpu.VMEM((n,) + tail, kind)

    def tiles(n, kind=BF16):
        return pltpu.VMEM((n, rows, rows), kind)

    def call(kernel, scalars, args, outs, scratch, flops, in_place=(), out_place=()):
        size = sum(a.size * a.dtype.itemsize for a in args)
        size += sum(o.size * o.dtype.itemsize for o in outs)
        return pl.pallas_call(
            kernel,
            out_shape=tuple(outs),
            in_specs=[SMEM] * len(scalars) + [VMEM if i in in_place else ANY for i in range(len(args))],
            out_specs=tuple(ANY if i in out_place else VMEM for i in range(len(outs))),
            scratch_shapes=scratch,
            cost_estimate=pl.CostEstimate(flops=flops, bytes_accessed=size, transcendentals=0),
        )(*scalars, *args)

    def sems(n):
        return pltpu.SemaphoreType.DMA((n,))

    tile_flops = 2 * rows * rows * width

    def split_shapes(n):
        return [blocks(n, BF16), blocks(n, BF16), blocks(n, BF16), blocks(n, F32)]

    def finished(own_part, arrived):
        n = own_part.shape[0]
        return call(finish_kernel, (), (own_part,) + arrived, [blocks(n, BF16)], [], 0, range(4))[0]

    part_feats = spread_relayed(feats)
    partner_feats = spread_relayed(swapped(feats, bits[2]))
    ids = swapped(sends, bits[2])

    deg, gh, z_next, z_far, z_before, z_own = call(
        degree_kernel, (counts, lrows, rrows, rslots, me), (lv, rv, go, weight),
        [jax.ShapeDtypeStruct((own, rows, rows), F32), blocks(own, BF16)] + split_shapes(share),
        [tiles(lcap), tiles(rounds * cap), room(own, BF16), tiles(own + 1, F32), room(cap + 1, F32), sems(3)],
        cap * tile_flops, (3,),
    )
    back_b, back_a = call(
        parcels_kernel, (counts, rrows, rslots), (rv, gh), [blocks(cap, BF16), blocks(cap, BF16)],
        [tiles(2 * cap), room(own, BF16), room(cap + 1, F32), sems(2)], 2 * cap * tile_flops,
    )
    z_arrived = scattered(z_next, z_far, z_before)
    got_back_b = swapped(back_b, bits[1])
    got_back_a = swapped(back_a, bits[0])
    got_back_c = swapped(finished(z_own, z_arrived), bits[2])

    need_a, need_b, near = call(
        feat_kernel, (counts, lrows, lcols, sends, me), part_feats + (lv,),
        [blocks(cap, BF16), blocks(cap, BF16), blocks(own, F32)],
        [room(part, BF16), tiles(lcap), room(own + 1, F32), sems(6), sems(cap), sems(cap)],
        lcap * tile_flops, (), range(2),
    )
    got_b = swapped(need_b, bits[1])
    got_a = swapped(need_a, bits[0])

    right, left, keep_r, keep_l, own_part = call(
        merge_kernel, (counts, lrows, lcols, sends, me), (lv, gh, got_back_a, got_back_b, got_back_c),
        [blocks(own, BF16), blocks(own, BF16), blocks(half, F32), blocks(half, F32), blocks(own, F32)],
        [tiles(lcap), room(own, BF16), room(cap, BF16), room(cap, BF16), room(share, BF16), room(part + 1, F32), sems(5)],
        lcap * tile_flops,
    )
    a_left = shifted(right, 1)
    a_right = shifted(left, -1)

    def halves(start):
        return pl.BlockSpec((half,) + tail, lambda i: (start, 0, 0))

    out_r, out_l = pl.pallas_call(
        combine_kernel,
        out_shape=(blocks(half, BF16), blocks(half, BF16)),
        grid=(1,),
        in_specs=[halves(0)] * 4,
        out_specs=(halves(0), halves(0)),
        cost_estimate=pl.CostEstimate(flops=0, bytes_accessed=8 * half * rows * width, transcendentals=0),
    )(keep_r, keep_l, a_left, a_right)
    b_left = shifted(out_r, 1)
    b_right = shifted(out_l, -1)
    grad_features = pl.pallas_call(
        relay_finish_kernel,
        out_shape=blocks(own, BF16),
        grid=(1,),
        in_specs=[pl.BlockSpec((own,) + tail, lambda i: (0, 0, 0)), halves(1), halves(1), halves(0), halves(0)],
        out_specs=pl.BlockSpec((own,) + tail, lambda i: (0, 0, 0)),
        cost_estimate=pl.CostEstimate(flops=0, bytes_accessed=10 * own * rows * width, transcendentals=0),
    )(own_part, a_left, a_right, b_left, b_right)

    mid = call(
        mid_kernel, (counts, rrows, rslots, ids, me), (got_a,) + partner_feats + (rv, near),
        [blocks(own, F32)],
        [room(cap + part, BF16), tiles(2 * cap), room(own + 1, F32), sems(9)], 2 * cap * tile_flops,
    )[0]
    output = call(
        far_kernel, (counts, rrows, rslots), (got_b, rv, mid, deg, weight), [blocks(own, BF16)],
        [room(cap, BF16), tiles(cap), room(own + 1, F32), tiles(own, F32), sems(4)], cap * tile_flops, (4,),
    )[0]
    return (output.reshape(rows_dev, width), grad_features.reshape(rows_dev, width))


def solution(mesh):
    in_specs = (
        P(("node", "feat"), None),
        P(),
        P(("node", "feat"), None),
        P("node", "feat", None),
        P("node", "feat", None),
        P("node", "feat", None, None, None),
        P("node", "feat", None, None),
        P("node", "feat", None, None),
        P("node", "feat", None, None, None, None),
        P("node", None, None),
        P("node", "feat", None),
    )
    out_specs = (P(("node", "feat"), None), P(("node", "feat"), None))
    return jax.shard_map(body, mesh=mesh, in_specs=in_specs, out_specs=out_specs, check_vma=False)
```

```python
import jax
import jax.numpy as jnp
from jax import lax
from jax.experimental import pallas as pl
from jax.experimental.pallas import tpu as pltpu
from jax.sharding import PartitionSpec as P


UNROLL = 4
VMEM_ALL = 67_043_328
F32 = jnp.float32
BF16 = jnp.bfloat16
SMEM = pl.BlockSpec(memory_space=pltpu.SMEM)
VMEM = pl.BlockSpec(memory_space=pltpu.VMEM)
ANY = pl.BlockSpec(memory_space=pl.ANY)
HBM = pl.BlockSpec(memory_space=pltpu.HBM)


def swapped(array, bit):
    return lax.ppermute(array, "node", [(i, i ^ 1 << bit) for i in range(lax.axis_size("node"))])


def shifted(array, step):
    size = lax.axis_size("feat")
    return lax.ppermute(array, "feat", [(i, (i + step) % size) for i in range(size)])


def spread_relayed(mine):
    half = mine.shape[0] // 2
    before = shifted(mine, 1)
    after = shifted(mine, -1)
    far_low = shifted(before[:half], 1)
    far_high = shifted(after[half:], -1)
    return (mine, after, far_low, far_high, before)


def scattered(to_next, to_far, to_before):
    return shifted(to_next, 1), shifted(to_far, 2), shifted(to_before, -1)


def start_all(pairs, sems):
    copies = [pltpu.make_async_copy(a, b, sems.at[i]) for i, (a, b) in enumerate(pairs)]
    for copy in copies:
        copy.start()
    return copies


def wait_all(copies):
    for copy in copies:
        copy.wait()


def pieces_into(pieces, dst, base):
    pairs = []
    for piece in pieces:
        pairs.append((piece, dst.at[pl.ds(base, piece.shape[0])]))
        base += piece.shape[0]
    return pairs


def for_live(count, step):
    def group(k, carry):
        for u in range(UNROLL):
            t = k * UNROLL + u
            step(t, t < count)
        return carry

    lax.fori_loop(0, pl.cdiv(count, UNROLL), group, 0)


def forward_tiles(count, base, vals, row_of, source_of, acc):
    trash = acc.shape[0] - 1

    def step(t, live):
        row = jnp.where(live, row_of(t), trash)
        acc[row] += jnp.dot(vals[base + t], source_of(t), preferred_element_type=F32)

    for_live(count, step)


def backward_tiles(count, base, vals, row_of, target_of, grads, acc):
    trash = acc.shape[0] - 1

    def step(t, live):
        target = jnp.where(live, target_of(t), trash)
        acc[target] += lax.dot_general(
            vals[base + t], grads[row_of(t)], (((0,), (0,)), ((), ())), preferred_element_type=F32
        )

    for_live(count, step)


def degree_kernel(counts, lrows, rrows, rslots, me, lv_hbm, rv_hbm, go_hbm, w_ref,
                  deg_ref, gh_ref, next_ref, far_ref, before_ref, own_ref,
                  lv, rv, go, dacc, acc, sems):
    copies = start_all([(lv_hbm, lv), (rv_hbm, rv), (go_hbm, go)], sems)
    own = deg_ref.shape[0]
    cap = rrows.shape[2]
    dacc[...] = jnp.zeros_like(dacc)
    acc[...] = jnp.zeros_like(acc)
    copies[0].wait()

    def add_rows(vals, base, row_of):
        def step(t, live):
            row = jnp.where(live, row_of(t), own)
            dacc[row] += vals[base + t].astype(F32)

        return step

    for_live(counts[0], add_rows(lv, 0, lambda t: lrows[t]))
    copies[1].wait()
    for r in range(rrows.shape[0]):
        for_live(counts[r + 1], add_rows(rv, r * cap, lambda t: rrows[r, 0, t]))
    copies[2].wait()
    for b in range(own):
        degree = 1.0 + jnp.broadcast_to(jnp.sum(dacc[b], axis=1, keepdims=True), dacc.shape[1:])
        deg_ref[b] = degree
        dense = lax.dot_general(go[b], w_ref[...], (((1,), (1,)), ((), ())), preferred_element_type=F32)
        width = degree.shape[1]
        for k in range(dense.shape[1] // width):
            gh_ref[b, :, k * width:(k + 1) * width] = (
                dense[:, k * width:(k + 1) * width] / degree
            ).astype(BF16)
    share = own_ref.shape[0]
    shift = me[0] * share
    backward_tiles(
        counts[3], 2 * cap, rv, lambda t: rrows[2, 0, t],
        lambda t: lax.rem(rslots[2, 0, t] - shift + cap, cap), gh_ref, acc,
    )
    split_out(acc, share, next_ref, far_ref, before_ref, own_ref)


def parcels_kernel(counts, rrows, rslots, rv_hbm, gh_hbm, out_b, out_a, rv, gh, acc, sems):
    cap = rrows.shape[2]
    copies = start_all([(rv_hbm.at[pl.ds(0, 2 * cap)], rv), (gh_hbm, gh)], sems)
    acc[...] = jnp.zeros_like(acc)
    wait_all(copies)
    for r, out in ((1, out_b), (0, out_a)):
        backward_tiles(
            counts[r + 1], r * cap, rv, lambda t: rrows[r, 0, t], lambda t: rslots[r, 0, t], gh, acc
        )
        out[...] = acc[:cap].astype(BF16)
        if r:
            acc[...] = jnp.zeros_like(acc)


def split_out(acc, n, next_ref, far_ref, before_ref, own_ref):
    next_ref[...] = acc[n:2 * n].astype(BF16)
    far_ref[...] = acc[2 * n:3 * n].astype(BF16)
    before_ref[...] = acc[3 * n:4 * n].astype(BF16)
    own_ref[...] = acc[:n]


def merge_kernel(counts, lrows, lcols, sends, me, lv_hbm, gh_hbm, a_hbm, b_hbm, c_hbm,
                 right_ref, left_ref, keep_r_ref, keep_l_ref, own_ref, lv, gh, got_a, got_b, got_c, acc, sems):
    copies = start_all([(lv_hbm, lv), (gh_hbm, gh), (a_hbm, got_a), (b_hbm, got_b), (c_hbm, got_c)], sems)
    own = gh.shape[0]
    total = acc.shape[0] - 1
    acc[own:] = jnp.zeros((total + 1 - own,) + acc.shape[1:], F32)
    wait_all(copies[:2])
    acc[:own] = gh[...].astype(F32)
    shift = me[0] * own
    backward_tiles(
        counts[0], 0, lv, lambda t: lrows[t],
        lambda t: lax.rem(lcols[t] - shift + total, total), gh, acc,
    )
    wait_all(copies[2:])
    for r, (got, base) in enumerate(((got_a, 0), (got_b, 0), (got_c, me[0] * got_c.shape[0]))):
        for s in range(got.shape[0]):
            acc[lax.rem(sends[r, 0, base + s] - shift + total, total)] += got[s].astype(F32)
    n, h = own, own // 2
    right_ref[:h] = acc[2 * n:2 * n + h].astype(BF16)
    right_ref[h:] = acc[n + h:2 * n].astype(BF16)
    left_ref[:h] = acc[2 * n + h:3 * n].astype(BF16)
    left_ref[h:] = acc[3 * n:3 * n + h].astype(BF16)
    keep_r_ref[...] = acc[n:n + h]
    keep_l_ref[...] = acc[3 * n + h:4 * n]
    own_ref[...] = acc[:n]


def combine_kernel(keep_r, keep_l, from_left, from_right, out_r, out_l, keep, came, sems):
    h = keep_r.shape[0]
    pairs = pieces_into((keep_r, keep_l), keep, 0)
    pairs += pieces_into((from_left.at[pl.ds(0, h)], from_right.at[pl.ds(0, h)]), came, 0)
    wait_all(start_all(pairs, sems))
    out_r[...] = (keep[:h] + came[:h].astype(F32)).astype(BF16)
    out_l[...] = (keep[h:] + came[h:].astype(F32)).astype(BF16)


def relay_finish_kernel(own_hbm, a_left, a_right, b_left, b_right, out, own, first, second, sems):
    h = out.shape[0] // 2
    pairs = [(own_hbm, own)]
    pairs += pieces_into((a_right.at[pl.ds(h, h)], a_left.at[pl.ds(h, h)]), first, 0)
    pairs += pieces_into((b_left, b_right), second, 0)
    wait_all(start_all(pairs, sems))
    out[...] = (own[...] + first[...].astype(F32) + second[...].astype(F32)).astype(BF16)


def finish_kernel(own_hbm, a_hbm, b_hbm, c_hbm, out, own, a, b, c, sems):
    wait_all(start_all([(own_hbm, own), (a_hbm, a), (b_hbm, b), (c_hbm, c)], sems))
    out[...] = (own[...] + a[...].astype(F32) + b[...].astype(F32) + c[...].astype(F32)).astype(BF16)


def pick_kernel(sends, me, p0, p1, p2, p3, p4, out_a, out_b, src, sems, sems_a, sems_b):
    wait_all(start_all(pieces_into((p0, p1, p2, p3, p4), src, 0), sems))
    total = src.shape[0]
    shift = me[0] * p0.shape[0]
    picks = ((out_b, 1, sems_b), (out_a, 0, sems_a))

    def begin(out, r, marks):
        def one(s, carry):
            at = lax.rem(sends[r, 0, s] - shift + total, total)
            pltpu.make_async_copy(src.at[at], out.at[s], marks.at[s]).start()
            return carry

        lax.fori_loop(0, out.shape[0], one, 0)

    def end(out, r, marks):
        def one(s, carry):
            pltpu.make_async_copy(src.at[0], out.at[s], marks.at[s]).wait()
            return carry

        lax.fori_loop(0, out.shape[0], one, 0)

    for pick in picks:
        begin(*pick)
    for pick in picks:
        end(*pick)


def near_kernel(counts, lrows, lcols, rrows, rslots, me, a_hbm, p0, p1, p2, p3, p4, lv_hbm, rv_hbm,
                out_ref, src, vals, acc, sems):
    own = out_ref.shape[0]
    cap = rrows.shape[2]
    lcap = vals.shape[0] - cap
    part = src.shape[0] - cap
    pairs = [(lv_hbm, vals.at[pl.ds(0, lcap)]), (rv_hbm.at[pl.ds(0, cap)], vals.at[pl.ds(lcap, cap)])]
    wait_all(start_all(pairs + pieces_into((p0, p1, p2, p3, p4, a_hbm), src, 0), sems))
    acc[:own] = src[:own].astype(F32)
    shift = me[0] * own
    forward_tiles(
        counts[0], 0, vals, lambda t: lrows[t], lambda t: src[lax.rem(lcols[t] - shift + part, part)], acc
    )
    forward_tiles(counts[1], lcap, vals, lambda t: rrows[0, 0, t], lambda t: src[part + rslots[0, 0, t]], acc)
    out_ref[...] = acc[:own]


def far_kernel(counts, rrows, rslots, ids, me, b_hbm, p0, p1, p2, p3, p4, rv_hbm, near_hbm, deg_hbm, w_ref,
               out_ref, src, vals, acc, deg, sems):
    total = out_ref.shape[0]
    cap = rrows.shape[2]
    part = src.shape[0] - cap
    pairs = [(near_hbm, acc.at[pl.ds(0, total)]), (rv_hbm.at[pl.ds(cap, 2 * cap)], vals)]
    pairs += pieces_into((b_hbm, p0, p1, p2, p3, p4), src, 0) + [(deg_hbm, deg)]
    wait_all(start_all(pairs, sems))
    forward_tiles(counts[2], 0, vals, lambda t: rrows[1, 0, t], lambda t: src[rslots[1, 0, t]], acc)
    shift = me[0] * p0.shape[0]
    forward_tiles(
        counts[3], cap, vals, lambda t: rrows[2, 0, t],
        lambda t: src[cap + lax.rem(ids[2, 0, rslots[2, 0, t]] - shift + part, part)], acc,
    )
    width = deg.shape[2]
    for b in range(total):
        hidden = jnp.concatenate(
            [acc[b, :, k:k + width] / deg[b] for k in range(0, acc.shape[2], width)], axis=1
        ).astype(BF16)
        out_ref[b] = jnp.dot(hidden, w_ref[...], preferred_element_type=F32).astype(BF16)


def body(
    features,
    weight,
    grad_out,
    local_rows,
    local_cols,
    local_values,
    remote_rows,
    remote_slots,
    remote_values,
    send_blocks,
    tile_counts,
):
    rows_dev, width = features.shape
    lcap, rows = local_values.shape[2:4]
    own = rows_dev // rows
    rounds, cap = remote_rows.shape[2:]
    slices = lax.axis_size("feat")
    part = own * slices
    share = cap // slices
    half = own // 2
    log_nodes = lax.axis_size("node").bit_length() - 1
    bits = [r * log_nodes // rounds for r in range(rounds)]
    tail = (rows, width)

    me = lax.axis_index("feat").astype(jnp.int32).reshape(1)
    counts = tile_counts[0, 0]
    lrows, lcols = local_rows[0, 0], local_cols[0, 0]
    rrows, rslots, sends = (a.reshape(rounds, 1, cap) for a in (remote_rows, remote_slots, send_blocks))
    lv = local_values.reshape(lcap, rows, rows)
    rv = remote_values.reshape(rounds * cap, rows, rows)
    feats = features.reshape((own,) + tail)
    go = grad_out.reshape((own,) + tail)

    def blocks(n, kind):
        return jax.ShapeDtypeStruct((n,) + tail, kind)

    def room(n, kind):
        return pltpu.VMEM((n,) + tail, kind)

    def tiles(n, kind=BF16):
        return pltpu.VMEM((n, rows, rows), kind)

    def call(kernel, scalars, args, outs, scratch, flops, in_place=(), out_place=(), held=()):
        size = sum(a.size * a.dtype.itemsize for a in args)
        size += sum(o.size * o.dtype.itemsize for o in outs)
        return pl.pallas_call(
            kernel,
            out_shape=tuple(outs),
            in_specs=[SMEM] * len(scalars) + [VMEM if i in in_place else HBM if i in held else ANY for i in range(len(args))],
            out_specs=tuple(ANY if i in out_place else VMEM for i in range(len(outs))),
            scratch_shapes=scratch,
            compiler_params=pltpu.CompilerParams(vmem_limit_bytes=VMEM_ALL),
            cost_estimate=pl.CostEstimate(flops=flops, bytes_accessed=size, transcendentals=0),
        )(*scalars, *args)

    def sems(n):
        return pltpu.SemaphoreType.DMA((n,))

    tile_flops = 2 * rows * rows * width

    def split_shapes(n):
        return [blocks(n, BF16), blocks(n, BF16), blocks(n, BF16), blocks(n, F32)]

    def finished(own_part, arrived):
        n = own_part.shape[0]
        return call(
            finish_kernel, (), (own_part,) + arrived, [blocks(n, BF16)],
            [room(n, F32), room(n, BF16), room(n, BF16), room(n, BF16), sems(4)], 0, held=range(4),
        )[0]

    part_feats = spread_relayed(feats)
    partner_feats = spread_relayed(swapped(feats, bits[2]))
    ids = swapped(sends, bits[2])

    deg, gh, z_next, z_far, z_before, z_own = call(
        degree_kernel, (counts, lrows, rrows, rslots, me), (lv, rv, go, weight),
        [jax.ShapeDtypeStruct((own, rows, rows), F32), blocks(own, BF16)] + split_shapes(share),
        [tiles(lcap), tiles(rounds * cap), room(own, BF16), tiles(own + 1, F32), room(cap + 1, F32), sems(3)],
        cap * tile_flops, (3,),
    )
    back_b, back_a = call(
        parcels_kernel, (counts, rrows, rslots), (rv, gh), [blocks(cap, BF16), blocks(cap, BF16)],
        [tiles(2 * cap), room(own, BF16), room(cap + 1, F32), sems(2)], 2 * cap * tile_flops,
    )
    z_arrived = scattered(z_next, z_far, z_before)
    got_back_b = swapped(back_b, bits[1])
    got_back_a = swapped(back_a, bits[0])
    got_back_c = swapped(finished(z_own, z_arrived), bits[2])

    need_a, need_b = call(
        pick_kernel, (sends, me), part_feats, [blocks(cap, BF16), blocks(cap, BF16)],
        [room(part, BF16), sems(5), sems(cap), sems(cap)], 0, out_place=range(2),
    )
    got_b = swapped(need_b, bits[1])
    got_a = swapped(need_a, bits[0])

    right, left, keep_r, keep_l, own_part = call(
        merge_kernel, (counts, lrows, lcols, sends, me), (lv, gh, got_back_a, got_back_b, got_back_c),
        [blocks(own, BF16), blocks(own, BF16), blocks(half, F32), blocks(half, F32), blocks(own, F32)],
        [tiles(lcap), room(own, BF16), room(cap, BF16), room(cap, BF16), room(share, BF16), room(part + 1, F32), sems(5)],
        lcap * tile_flops, held=range(5),
    )
    a_left = shifted(right, 1)
    a_right = shifted(left, -1)

    out_r, out_l = call(
        combine_kernel, (), (keep_r, keep_l, a_left, a_right), [blocks(half, BF16), blocks(half, BF16)],
        [room(own, F32), room(own, BF16), sems(4)], 0, held=range(4),
    )
    b_left = shifted(out_r, 1)
    b_right = shifted(out_l, -1)
    grad_features = call(
        relay_finish_kernel, (), (own_part, a_left, a_right, b_left, b_right), [blocks(own, BF16)],
        [room(own, F32), room(own, BF16), room(own, BF16), sems(5)], 0, held=range(5),
    )[0]

    near = call(
        near_kernel, (counts, lrows, lcols, rrows, rslots, me), (got_a,) + part_feats + (lv, rv),
        [blocks(own, F32)],
        [room(part + cap, BF16), tiles(lcap + cap), room(own + 1, F32), sems(8)], (lcap + cap) * tile_flops,
    )[0]
    output = call(
        far_kernel, (counts, rrows, rslots, ids, me), (got_b,) + partner_feats + (rv, near, deg, weight),
        [blocks(own, BF16)],
        [room(cap + part, BF16), tiles(2 * cap), room(own + 1, F32), tiles(own, F32), sems(9)],
        2 * cap * tile_flops, (9,),
    )[0]
    return (output.reshape(rows_dev, width), grad_features.reshape(rows_dev, width))


def solution(mesh):
    in_specs = (
        P(("node", "feat"), None),
        P(),
        P(("node", "feat"), None),
        P("node", "feat", None),
        P("node", "feat", None),
        P("node", "feat", None, None, None),
        P("node", "feat", None, None),
        P("node", "feat", None, None),
        P("node", "feat", None, None, None, None),
        P("node", None, None),
        P("node", "feat", None),
    )
    out_specs = (P(("node", "feat"), None), P(("node", "feat"), None))
    return jax.shard_map(body, mesh=mesh, in_specs=in_specs, out_specs=out_specs, check_vma=False)
```

```python
import jax
import jax.numpy as jnp
from jax import lax
from jax.experimental import pallas as pl
from jax.experimental.pallas import tpu as pltpu
from jax.sharding import PartitionSpec as P


UNROLL = 8
VMEM_ALL = 67_043_328
F32 = jnp.float32
BF16 = jnp.bfloat16
SMEM = pl.BlockSpec(memory_space=pltpu.SMEM)
VMEM = pl.BlockSpec(memory_space=pltpu.VMEM)
ANY = pl.BlockSpec(memory_space=pl.ANY)
HBM = pl.BlockSpec(memory_space=pltpu.HBM)


def swapped(array, bit):
    return lax.ppermute(array, "node", [(i, i ^ 1 << bit) for i in range(lax.axis_size("node"))])


def shifted(array, step):
    size = lax.axis_size("feat")
    return lax.ppermute(array, "feat", [(i, (i + step) % size) for i in range(size)])


def relay_begun(mine):
    return shifted(mine, 1), shifted(mine, -1)


def relayed(mine, before, after, low, high):
    return (mine, after, shifted(low, 1), shifted(high, -1), before)


def scattered(to_next, to_far, to_before):
    return shifted(to_next, 1), shifted(to_far, 2), shifted(to_before, -1)


def start_all(pairs, sems):
    copies = [pltpu.make_async_copy(a, b, sems.at[i]) for i, (a, b) in enumerate(pairs)]
    for copy in copies:
        copy.start()
    return copies


def wait_all(copies):
    for copy in copies:
        copy.wait()


def pieces_into(pieces, dst, base):
    pairs = []
    for piece in pieces:
        pairs.append((piece, dst.at[pl.ds(base, piece.shape[0])]))
        base += piece.shape[0]
    return pairs


def for_live(count, step):
    def group(k, carry):
        for u in range(UNROLL):
            t = k * UNROLL + u
            step(t, t < count)
        return carry

    lax.fori_loop(0, pl.cdiv(count, UNROLL), group, 0)


def forward_tiles(count, base, vals, row_of, source_of, acc):
    trash = acc.shape[0] - 1

    def step(t, live):
        row = jnp.where(live, row_of(t), trash)
        acc[row] += jnp.dot(vals[base + t], source_of(t), preferred_element_type=F32)

    for_live(count, step)


def backward_tiles(count, base, vals, row_of, target_of, grads, acc):
    trash = acc.shape[0] - 1

    def step(t, live):
        target = jnp.where(live, target_of(t), trash)
        acc[target] += lax.dot_general(
            vals[base + t], grads[row_of(t)], (((0,), (0,)), ((), ())), preferred_element_type=F32
        )

    for_live(count, step)


def degree_kernel(counts, lrows, rrows, rslots, me, lv_hbm, rv_hbm, go_hbm, w_ref,
                  deg_ref, gh_ref, next_ref, far_ref, before_ref, own_ref,
                  lv, rv, go, dacc, acc, sems):
    copies = start_all([(lv_hbm, lv), (rv_hbm, rv), (go_hbm, go)], sems)
    own = deg_ref.shape[0]
    cap = rrows.shape[2]
    dacc[...] = jnp.zeros_like(dacc)
    acc[...] = jnp.zeros_like(acc)
    copies[0].wait()

    def add_rows(vals, base, row_of):
        def step(t, live):
            row = jnp.where(live, row_of(t), own)
            dacc[row] += vals[base + t].astype(F32)

        return step

    for_live(counts[0], add_rows(lv, 0, lambda t: lrows[t]))
    copies[1].wait()
    for r in range(rrows.shape[0]):
        for_live(counts[r + 1], add_rows(rv, r * cap, lambda t: rrows[r, 0, t]))
    copies[2].wait()
    for b in range(own):
        degree = 1.0 + jnp.broadcast_to(jnp.sum(dacc[b], axis=1, keepdims=True), dacc.shape[1:])
        deg_ref[b] = degree
        dense = lax.dot_general(go[b], w_ref[...], (((1,), (1,)), ((), ())), preferred_element_type=F32)
        width = degree.shape[1]
        for k in range(dense.shape[1] // width):
            gh_ref[b, :, k * width:(k + 1) * width] = (
                dense[:, k * width:(k + 1) * width] / degree
            ).astype(BF16)
    share = own_ref.shape[0]
    shift = me[0] * share
    backward_tiles(
        counts[3], 2 * cap, rv, lambda t: rrows[2, 0, t],
        lambda t: lax.rem(rslots[2, 0, t] - shift + cap, cap), gh_ref, acc,
    )
    split_out(acc, share, next_ref, far_ref, before_ref, own_ref)


def parcels_kernel(counts, rrows, rslots, rv_hbm, gh_hbm, out_b, out_a, rv, gh, acc, sems):
    cap = rrows.shape[2]
    copies = start_all([(rv_hbm.at[pl.ds(0, 2 * cap)], rv), (gh_hbm, gh)], sems)
    acc[...] = jnp.zeros_like(acc)
    wait_all(copies)
    for r, out in ((1, out_b), (0, out_a)):
        backward_tiles(
            counts[r + 1], r * cap, rv, lambda t: rrows[r, 0, t], lambda t: rslots[r, 0, t], gh, acc
        )
        out[...] = acc[:cap].astype(BF16)
        if r:
            acc[...] = jnp.zeros_like(acc)


def split_out(acc, n, next_ref, far_ref, before_ref, own_ref):
    next_ref[...] = acc[n:2 * n].astype(BF16)
    far_ref[...] = acc[2 * n:3 * n].astype(BF16)
    before_ref[...] = acc[3 * n:4 * n].astype(BF16)
    own_ref[...] = acc[:n]


def halves(before, after, low, high):
    h = low.shape[0]
    return [(before.at[pl.ds(0, h)], low), (after.at[pl.ds(h, h)], high)]


def cut_kernel(before, after, low, high, sems):
    wait_all(start_all(halves(before, after, low, high), sems))


def merge_kernel(counts, lrows, lcols, sends, me, lv_hbm, gh_hbm, a_hbm, b_hbm, c_hbm, before, after,
                 right_ref, left_ref, keep_r_ref, keep_l_ref, own_ref, low, high,
                 lv, gh, got_a, got_b, got_c, acc, sems, sems_cut):
    cuts = start_all(halves(before, after, low, high), sems_cut)
    copies = start_all([(lv_hbm, lv), (gh_hbm, gh), (a_hbm, got_a), (b_hbm, got_b), (c_hbm, got_c)], sems)
    own = gh.shape[0]
    total = acc.shape[0] - 1
    acc[own:] = jnp.zeros((total + 1 - own,) + acc.shape[1:], F32)
    wait_all(copies[:2])
    acc[:own] = gh[...].astype(F32)
    shift = me[0] * own
    backward_tiles(
        counts[0], 0, lv, lambda t: lrows[t],
        lambda t: lax.rem(lcols[t] - shift + total, total), gh, acc,
    )
    wait_all(copies[2:])
    for r, (got, base) in enumerate(((got_a, 0), (got_b, 0), (got_c, me[0] * got_c.shape[0]))):
        for s in range(got.shape[0]):
            acc[lax.rem(sends[r, 0, base + s] - shift + total, total)] += got[s].astype(F32)
    n, h = own, own // 2
    right_ref[:h] = acc[2 * n:2 * n + h].astype(BF16)
    right_ref[h:] = acc[n + h:2 * n].astype(BF16)
    left_ref[:h] = acc[2 * n + h:3 * n].astype(BF16)
    left_ref[h:] = acc[3 * n:3 * n + h].astype(BF16)
    keep_r_ref[...] = acc[n:n + h]
    keep_l_ref[...] = acc[3 * n + h:4 * n]
    own_ref[...] = acc[:n]
    wait_all(cuts)


def combine_kernel(keep_r, keep_l, from_left, from_right, out_r, out_l, keep, came, sems):
    h = keep_r.shape[0]
    pairs = pieces_into((keep_r, keep_l), keep, 0)
    pairs += pieces_into((from_left.at[pl.ds(0, h)], from_right.at[pl.ds(0, h)]), came, 0)
    wait_all(start_all(pairs, sems))
    out_r[...] = (keep[:h] + came[:h].astype(F32)).astype(BF16)
    out_l[...] = (keep[h:] + came[h:].astype(F32)).astype(BF16)


def relay_finish_kernel(own_hbm, a_left, a_right, b_left, b_right, out, own, first, second, sems):
    h = out.shape[0] // 2
    pairs = [(own_hbm, own)]
    pairs += pieces_into((a_right.at[pl.ds(h, h)], a_left.at[pl.ds(h, h)]), first, 0)
    pairs += pieces_into((b_left, b_right), second, 0)
    wait_all(start_all(pairs, sems))
    out[...] = (own[...] + first[...].astype(F32) + second[...].astype(F32)).astype(BF16)


def finish_kernel(own_hbm, a_hbm, b_hbm, c_hbm, out, own, a, b, c, sems):
    wait_all(start_all([(own_hbm, own), (a_hbm, a), (b_hbm, b), (c_hbm, c)], sems))
    out[...] = (own[...] + a[...].astype(F32) + b[...].astype(F32) + c[...].astype(F32)).astype(BF16)


def pick_kernel(sends, me, p0, p1, p2, p3, p4, out_a, out_b, src, sems, sems_a, sems_b):
    wait_all(start_all(pieces_into((p0, p1, p2, p3, p4), src, 0), sems))
    total = src.shape[0]
    shift = me[0] * p0.shape[0]
    picks = ((out_b, 1, sems_b), (out_a, 0, sems_a))

    def begin(out, r, marks):
        def one(s, carry):
            at = lax.rem(sends[r, 0, s] - shift + total, total)
            pltpu.make_async_copy(src.at[at], out.at[s], marks.at[s]).start()
            return carry

        lax.fori_loop(0, out.shape[0], one, 0)

    def end(out, r, marks):
        def one(s, carry):
            pltpu.make_async_copy(src.at[0], out.at[s], marks.at[s]).wait()
            return carry

        lax.fori_loop(0, out.shape[0], one, 0)

    for pick in picks:
        begin(*pick)
    for pick in picks:
        end(*pick)


def near_kernel(counts, lrows, lcols, rrows, rslots, me, a_hbm, p0, p1, p2, p3, p4, lv_hbm, rv_hbm,
                out_ref, src, vals, acc, sems):
    own = out_ref.shape[0]
    cap = rrows.shape[2]
    lcap = vals.shape[0] - cap
    part = src.shape[0] - cap
    pairs = [(lv_hbm, vals.at[pl.ds(0, lcap)]), (rv_hbm.at[pl.ds(0, cap)], vals.at[pl.ds(lcap, cap)])]
    wait_all(start_all(pairs + pieces_into((p0, p1, p2, p3, p4, a_hbm), src, 0), sems))
    acc[:own] = src[:own].astype(F32)
    shift = me[0] * own
    forward_tiles(
        counts[0], 0, vals, lambda t: lrows[t], lambda t: src[lax.rem(lcols[t] - shift + part, part)], acc
    )
    forward_tiles(counts[1], lcap, vals, lambda t: rrows[0, 0, t], lambda t: src[part + rslots[0, 0, t]], acc)
    out_ref[...] = acc[:own]


def far_kernel(counts, rrows, rslots, ids, me, b_hbm, p0, p1, p2, p3, p4, rv_hbm, near_hbm, deg_hbm, w_ref,
               out_ref, src, vals, acc, deg, sems):
    total = out_ref.shape[0]
    cap = rrows.shape[2]
    part = src.shape[0] - cap
    pairs = [(near_hbm, acc.at[pl.ds(0, total)]), (rv_hbm.at[pl.ds(cap, 2 * cap)], vals)]
    pairs += pieces_into((b_hbm, p0, p1, p2, p3, p4), src, 0) + [(deg_hbm, deg)]
    wait_all(start_all(pairs, sems))
    forward_tiles(counts[2], 0, vals, lambda t: rrows[1, 0, t], lambda t: src[rslots[1, 0, t]], acc)
    shift = me[0] * p0.shape[0]
    forward_tiles(
        counts[3], cap, vals, lambda t: rrows[2, 0, t],
        lambda t: src[cap + lax.rem(ids[2, 0, rslots[2, 0, t]] - shift + part, part)], acc,
    )
    width = deg.shape[2]
    for b in range(total):
        hidden = jnp.concatenate(
            [acc[b, :, k:k + width] / deg[b] for k in range(0, acc.shape[2], width)], axis=1
        ).astype(BF16)
        out_ref[b] = jnp.dot(hidden, w_ref[...], preferred_element_type=F32).astype(BF16)


def body(
    features,
    weight,
    grad_out,
    local_rows,
    local_cols,
    local_values,
    remote_rows,
    remote_slots,
    remote_values,
    send_blocks,
    tile_counts,
):
    rows_dev, width = features.shape
    lcap, rows = local_values.shape[2:4]
    own = rows_dev // rows
    rounds, cap = remote_rows.shape[2:]
    slices = lax.axis_size("feat")
    part = own * slices
    share = cap // slices
    half = own // 2
    log_nodes = lax.axis_size("node").bit_length() - 1
    bits = [r * log_nodes // rounds for r in range(rounds)]
    tail = (rows, width)

    me = lax.axis_index("feat").astype(jnp.int32).reshape(1)
    counts = tile_counts[0, 0]
    lrows, lcols = local_rows[0, 0], local_cols[0, 0]
    rrows, rslots, sends = (a.reshape(rounds, 1, cap) for a in (remote_rows, remote_slots, send_blocks))
    lv = local_values.reshape(lcap, rows, rows)
    rv = remote_values.reshape(rounds * cap, rows, rows)
    feats = features.reshape((own,) + tail)
    go = grad_out.reshape((own,) + tail)

    def blocks(n, kind):
        return jax.ShapeDtypeStruct((n,) + tail, kind)

    def room(n, kind):
        return pltpu.VMEM((n,) + tail, kind)

    def tiles(n, kind=BF16):
        return pltpu.VMEM((n, rows, rows), kind)

    def call(kernel, scalars, args, outs, scratch, flops, in_place=(), out_place=(), held=()):
        size = sum(a.size * a.dtype.itemsize for a in args)
        size += sum(o.size * o.dtype.itemsize for o in outs)
        return pl.pallas_call(
            kernel,
            out_shape=tuple(outs),
            in_specs=[SMEM] * len(scalars) + [VMEM if i in in_place else HBM if i in held else ANY for i in range(len(args))],
            out_specs=tuple(ANY if i in out_place else VMEM for i in range(len(outs))),
            scratch_shapes=scratch,
            compiler_params=pltpu.CompilerParams(vmem_limit_bytes=VMEM_ALL),
            cost_estimate=pl.CostEstimate(flops=flops, bytes_accessed=size, transcendentals=0),
        )(*scalars, *args)

    def sems(n):
        return pltpu.SemaphoreType.DMA((n,))

    tile_flops = 2 * rows * rows * width

    def split_shapes(n):
        return [blocks(n, BF16), blocks(n, BF16), blocks(n, BF16), blocks(n, F32)]

    def finished(own_part, arrived):
        n = own_part.shape[0]
        return call(
            finish_kernel, (), (own_part,) + arrived, [blocks(n, BF16)],
            [room(n, F32), room(n, BF16), room(n, BF16), room(n, BF16), sems(4)], 0, held=range(4),
        )[0]

    before, after = relay_begun(feats)
    low, high = call(
        cut_kernel, (), (before, after), [blocks(half, BF16), blocks(half, BF16)], [sems(2)], 0, held=range(2)
    )
    part_feats = relayed(feats, before, after, low, high)
    partner = swapped(feats, bits[2])
    partner_before, partner_after = relay_begun(partner)
    ids = swapped(sends, bits[2])

    deg, gh, z_next, z_far, z_before, z_own = call(
        degree_kernel, (counts, lrows, rrows, rslots, me), (lv, rv, go, weight),
        [jax.ShapeDtypeStruct((own, rows, rows), F32), blocks(own, BF16)] + split_shapes(share),
        [tiles(lcap), tiles(rounds * cap), room(own, BF16), tiles(own + 1, F32), room(cap + 1, F32), sems(3)],
        cap * tile_flops, (3,),
    )
    back_b, back_a = call(
        parcels_kernel, (counts, rrows, rslots), (rv, gh), [blocks(cap, BF16), blocks(cap, BF16)],
        [tiles(2 * cap), room(own, BF16), room(cap + 1, F32), sems(2)], 2 * cap * tile_flops,
    )
    z_arrived = scattered(z_next, z_far, z_before)
    got_back_b = swapped(back_b, bits[1])
    got_back_a = swapped(back_a, bits[0])
    got_back_c = swapped(finished(z_own, z_arrived), bits[2])

    need_a, need_b = call(
        pick_kernel, (sends, me), part_feats, [blocks(cap, BF16), blocks(cap, BF16)],
        [room(part, BF16), sems(5), sems(cap), sems(cap)], 0, out_place=range(2),
    )
    got_b = swapped(need_b, bits[1])
    got_a = swapped(need_a, bits[0])

    right, left, keep_r, keep_l, own_part, low, high = call(
        merge_kernel, (counts, lrows, lcols, sends, me),
        (lv, gh, got_back_a, got_back_b, got_back_c, partner_before, partner_after),
        [blocks(own, BF16), blocks(own, BF16), blocks(half, F32), blocks(half, F32), blocks(own, F32)]
        + [blocks(half, BF16), blocks(half, BF16)],
        [tiles(lcap), room(own, BF16), room(cap, BF16), room(cap, BF16), room(share, BF16), room(part + 1, F32), sems(5), sems(2)],
        lcap * tile_flops, held=range(7),
    )
    partner_feats = relayed(partner, partner_before, partner_after, low, high)
    a_left = shifted(right, 1)
    a_right = shifted(left, -1)

    out_r, out_l = call(
        combine_kernel, (), (keep_r, keep_l, a_left, a_right), [blocks(half, BF16), blocks(half, BF16)],
        [room(own, F32), room(own, BF16), sems(4)], 0, held=range(4),
    )
    b_left = shifted(out_r, 1)
    b_right = shifted(out_l, -1)
    grad_features = call(
        relay_finish_kernel, (), (own_part, a_left, a_right, b_left, b_right), [blocks(own, BF16)],
        [room(own, F32), room(own, BF16), room(own, BF16), sems(5)], 0, held=range(5),
    )[0]

    near = call(
        near_kernel, (counts, lrows, lcols, rrows, rslots, me), (got_a,) + part_feats + (lv, rv),
        [blocks(own, F32)],
        [room(part + cap, BF16), tiles(lcap + cap), room(own + 1, F32), sems(8)], (lcap + cap) * tile_flops,
    )[0]
    output = call(
        far_kernel, (counts, rrows, rslots, ids, me), (got_b,) + partner_feats + (rv, near, deg, weight),
        [blocks(own, BF16)],
        [room(cap + part, BF16), tiles(2 * cap), room(own + 1, F32), tiles(own, F32), sems(9)],
        2 * cap * tile_flops, (9,),
    )[0]
    return (output.reshape(rows_dev, width), grad_features.reshape(rows_dev, width))


def solution(mesh):
    in_specs = (
        P(("node", "feat"), None),
        P(),
        P(("node", "feat"), None),
        P("node", "feat", None),
        P("node", "feat", None),
        P("node", "feat", None, None, None),
        P("node", "feat", None, None),
        P("node", "feat", None, None),
        P("node", "feat", None, None, None, None),
        P("node", None, None),
        P("node", "feat", None),
    )
    out_specs = (P(("node", "feat"), None), P(("node", "feat"), None))
    return jax.shard_map(body, mesh=mesh, in_specs=in_specs, out_specs=out_specs, check_vma=False)
```
